256 devices in a mesh: section: 2 (over z_lo), tile: 128 (over y, x, z_hi, core).
Axes of the slice: x: 4, y: 4, z: 8 (z_hi: 4, z_lo: 2; z = z_hi * 2 + z_lo), core: 2. Of those that a mesh axis runs over, the one named last changes fastest.
Arguments:
- features: bfloat16 [128, 12, 1024, 128], P('tile', 'section'), may hold values from -6 to 6
- conv_weight: bfloat16 [5, 5, 128, 128], replicated, may hold values from -0.109375 to 0.109375
- head_weight: bfloat16 [128, 16], replicated, may hold values from -0.5 to 0.5
- kernels: bfloat16 [128, 1024, 2048], P('tile'), may hold values from -0.015625 to 0.015625
- source_weights: float32 [8], replicated, may hold values from 0.3 to 3
Outputs:
- intensity: float32 [128, 12, 1024], P('tile', 'section')
The draws below stay inside these ranges and needn't reach their ends.
All inputs are finite; a program needn't handle non-finite values.
Results may differ from the reference program's by a relative error of at most 0.0018.
Values may be sent and summed in bfloat16 or wider, within the bound.
No kernel may reach another device: no remote copies, remote signals or barrier semaphores. Data moves between devices by JAX's collectives and lax.ppermute only.
A program may use at most 64 MiB of HBM per device.

```python
import math
import jax
import jax.numpy as jnp
from jax import lax

C = 128
K = 16
ANG = 8
W = 1024
TILES = 128
ROWS = 12


def steps_of(stream_key, shape, split, least, largest):
    gain = 1.0
    for axis_at, shards_of in split:
        draws = jax.random.uniform(jax.random.fold_in(jax.random.fold_in(stream_key, 6), axis_at), (shards_of,), jnp.float32, least / len(split), largest / len(split))
        gain = gain * jnp.repeat(jnp.exp(draws), shape[axis_at] // shards_of).reshape((-1,) + (1,) * (len(shape) - 1 - axis_at))
    return gain


def centred(rng, extent, scale, bound, shards=(), held_as=jnp.bfloat16):
    values = scale * jax.random.normal(rng, extent, jnp.float32)
    if shards:
        values = values * steps_of(rng, extent, shards, -0.22, 0.18)
    return jnp.clip(values, -bound, bound).astype(held_as)


def setup_inputs(seed: int = 0) -> dict:
    keys = jax.random.split(jax.random.key(seed), 6)
    return {
        "features": centred(keys[0], (TILES, ROWS, W, C), 1.0, 6.0, ((0, 128), (1, 2))),
        "conv_weight": centred(keys[1], (5, 5, C, C), (25 * C) ** -0.5, 0.109375),
        "head_weight": centred(keys[2], (C, 2 * ANG), C ** -0.5, 0.5),
        "kernels": centred(keys[3], (ANG * K, W, 2 * W), (W * K * ANG) ** -0.5, 0.015625, ((0, 128),)),
        "source_weights": jnp.clip(jnp.exp(jax.random.uniform(keys[4], (ANG,), jnp.float32, math.log(0.3), math.log(3.0))), 0.3, 3.0),
    }


def socs_image(field, operators):
    pixels = field.shape[-1]
    product = jnp.einsum('prw,kwv->pkrv', field.astype(jnp.float32), operators.astype(jnp.float32))
    real_part = product[0, :, :, :pixels] - product[1, :, :, pixels:]
    imag_part = product[0, :, :, pixels:] + product[1, :, :, :pixels]
    return jnp.sum(real_part * real_part + imag_part * imag_part, axis=0)


def reference(features, conv_weight, head_weight, kernels, source_weights):
    operators = kernels.reshape(ANG, K, kernels.shape[1], kernels.shape[2])

    def one_tile(window):
        preact = lax.conv_general_dilated(window[None], conv_weight, (1, 1), ((4, 4), (4, 4)), rhs_dilation=(2, 2), dimension_numbers=('NHWC', 'HWIO', 'NHWC'), preferred_element_type=jnp.float32)[0]
        hidden = jax.nn.gelu(preact, approximate=True).astype(jnp.bfloat16)
        near_field = jnp.einsum('rwc,cd->drw', hidden.astype(jnp.float32), head_weight.astype(jnp.float32)).astype(jnp.bfloat16)
        near_field = near_field.reshape(ANG, 2, near_field.shape[1], near_field.shape[2])
        running = jnp.zeros(near_field.shape[2:], jnp.float32)
        for angle_id in range(ANG):
            running = running + source_weights[angle_id] * socs_image(near_field[angle_id], operators[angle_id])
        return running
    return lax.map(one_tile, features)
```

```python
import jax
import jax.numpy as jnp
from jax import lax
from jax.sharding import Mesh, PartitionSpec as P

ANG = 8
TILE = ("y", "xh", "xl", "z", "c")


def padded_2(block, axis, dim, width):
    low = lax.ppermute(
        lax.slice_in_dim(block, block.shape[dim] - width, None, axis=dim), axis, [(0, 1)]
    )
    high = lax.ppermute(lax.slice_in_dim(block, 0, width, axis=dim), axis, [(1, 0)])
    return jnp.concatenate([low, block, high], axis=dim)


def on_device(features, conv_weight, head_weight, kernels, source_weights):
    pixels = features.shape[2]
    rows = features.shape[1]
    angle = lax.axis_index(("y", "xh"))
    weight = lax.dynamic_index_in_dim(source_weights, angle, 0, keepdims=False)
    swap = [(0, 1), (1, 0)]
    both = jnp.concatenate([kernels, lax.ppermute(kernels, "c", swap)], axis=0)
    padded = padded_2(features, "s", 1, 4)
    preact = lax.conv_general_dilated(
        padded,
        conv_weight,
        (1, 1),
        ((0, 0), (4, 4)),
        rhs_dilation=(2, 2),
        dimension_numbers=("NHWC", "HWIO", "NHWC"),
        preferred_element_type=jnp.float32,
    )
    hidden = jax.nn.gelu(preact, approximate=True).astype(jnp.bfloat16)
    near = jnp.einsum(
        "rwc,cd->drw", hidden[0], head_weight, preferred_element_type=jnp.float32
    ).astype(jnp.bfloat16)
    near = near.reshape(ANG, 2, rows, pixels)
    field = lax.all_to_all(near, ("y", "xh"), 0, 0, tiled=True)
    field = lax.all_gather(field, "z", axis=1, tiled=False)
    other = lax.ppermute(field, "xl", swap)

    def image(part):
        product = jnp.einsum(
            "azprw,kwv->pkazrv", part, both, preferred_element_type=jnp.float32
        )
        re = product[0, ..., :pixels] - product[1, ..., pixels:]
        im = product[0, ..., pixels:] + product[1, ..., :pixels]
        return weight * jnp.sum(re * re + im * im, axis=0)

    sent = lax.ppermute(image(other).astype(jnp.bfloat16), "xl", swap)
    total = image(field) + sent.astype(jnp.float32)
    total = total.astype(jnp.bfloat16).reshape(-1, rows, pixels)
    pieces = lax.all_to_all(total, ("y", "xh", "z"), 0, 0, tiled=True)
    return jnp.sum(pieces.astype(jnp.float32), axis=0, keepdims=True)


def solution(mesh):
    fine = Mesh(mesh.devices.reshape(2, 4, 2, 2, 4, 2), ("s",) + TILE)
    in_specs = (P(TILE, "s", None, None), P(), P(), P(TILE, None, None), P())
    return jax.shard_map(
        on_device, mesh=fine, in_specs=in_specs, out_specs=P(TILE, "s", None), check_vma=False
    )
```

```python
import functools

import jax
import jax.numpy as jnp
from jax import lax
from jax.experimental import pallas as pl
from jax.experimental.pallas import tpu as pltpu
from jax.sharding import Mesh, PartitionSpec as P

ANG = 8
TILE = ("y", "xh", "xl", "z", "c")
SWAP = [(0, 1), (1, 0)]
BF = jnp.bfloat16
F32 = jnp.float32


def sources(out):
    return [(e, (e - out) // 2 + 2) for e in range(out - 4, out + 5, 2) if e >= 0]


def conv_kernel(outs, rows, pixels, block, flip_ref, *refs):
    remotes, (w_ref, h_ref, o_ref, xp) = refs[1:-4], refs[-4:]
    x_ref = refs[0]
    flip = flip_ref[0]
    taps = w_ref.shape[0]
    used = sorted({e for o in outs for e, _ in sources(o)})
    xp[:, 0:8, :] = jnp.zeros((len(used), 8, xp.shape[2]), xp.dtype)
    xp[:, pixels + 8 :, :] = jnp.zeros((len(used), 8, xp.shape[2]), xp.dtype)
    for slot, e in enumerate(used):
        if e < rows:
            row = x_ref[e + flip * (rows - 1 - 2 * e)]
        else:
            at = (e - rows) % 2
            row = remotes[(e - rows) // 2][at + flip * (1 - 2 * at)]
        xp[slot, 8 : pixels + 8, :] = row
    for i, o in enumerate(outs):
        for m in range(0, pixels, block):
            acc = jnp.zeros((block, w_ref.shape[2]), F32)
            for e, d in sources(o):
                slot = used.index(e)
                left = jnp.concatenate(
                    [xp[slot, m + 4 + 2 * j : m + 4 + 2 * j + block, :] for j in range(taps)], axis=1
                )
                acc += jnp.dot(left, w_ref[d + flip * (4 - 2 * d)], preferred_element_type=F32)
            hidden = jax.nn.gelu(acc, approximate=True).astype(BF)
            near = lax.dot_general(
                h_ref[...], hidden, (((1,), (1,)), ((), ())), preferred_element_type=F32
            )
            o_ref[i, :, m : m + block] = near.astype(BF)


def near_rows(outs, flip, features, remotes, weights, head):
    rows, pixels, channels = features.shape
    used = sorted({e for o in outs for e, _ in sources(o)})
    flops = sum(len(sources(o)) for o in outs) * 2 * pixels * weights.shape[1] * channels
    vmem = pl.BlockSpec(memory_space=pltpu.VMEM)
    return pl.pallas_call(
        functools.partial(conv_kernel, outs, rows, pixels, 256),
        out_shape=jax.ShapeDtypeStruct((len(outs), head.shape[0], pixels), BF),
        in_specs=[pl.BlockSpec(memory_space=pltpu.SMEM)] + [vmem] * (3 + len(remotes)),
        out_specs=vmem,
        scratch_shapes=[pltpu.VMEM((len(used), pixels + 16, channels), BF)],
        compiler_params=pltpu.CompilerParams(vmem_limit_bytes=24 << 20),
        cost_estimate=pl.CostEstimate(
            flops=2 * flops, bytes_accessed=4 << 20, transcendentals=len(outs) * pixels * channels
        ),
        name="near_rows",
    )(flip, features, *remotes, weights, head)


def on_device(features, conv_weight, head_weight, kernels, source_weights):
    rows, pixels, channels = features.shape[1:]
    angle = lax.axis_index(("y", "xh"))
    section = lax.axis_index("s")
    weight = lax.dynamic_index_in_dim(source_weights, angle, 0, keepdims=False)
    window = features[0]
    edge = lax.dynamic_slice_in_dim(window, (1 - section) * (rows - 2), 2, 0)
    remote1 = lax.ppermute(edge, "s", SWAP)
    remote2 = lax.ppermute(window[2:4], "s", SWAP)
    both = jnp.concatenate([kernels, lax.ppermute(kernels, "c", SWAP)], axis=0)
    flip = section.astype(jnp.int32).reshape(1)
    taps = conv_weight.reshape(conv_weight.shape[0], -1, channels)
    head = head_weight.T
    near = jnp.concatenate(
        [
            near_rows((0, 1), flip, window, [], taps, head),
            near_rows((2, 3), flip, window, [remote1], taps, head),
            near_rows((4, 5), flip, window, [remote1, remote2], taps, head),
        ],
        axis=0,
    )
    near = near.reshape(rows, ANG, 2, pixels).transpose(1, 2, 0, 3)
    field = lax.all_to_all(near, ("y", "xh"), 0, 0, tiled=True)
    field = lax.all_gather(field, "z", axis=1, tiled=False)
    other = lax.ppermute(field, "xl", SWAP)

    def image(part):
        product = jnp.einsum(
            "azprw,kwv->pkazrv", part, both, preferred_element_type=jnp.float32
        )
        re = product[0, ..., :pixels] - product[1, ..., pixels:]
        im = product[0, ..., pixels:] + product[1, ..., :pixels]
        return weight * jnp.sum(re * re + im * im, axis=0)

    sent = lax.ppermute(image(other).astype(BF), "xl", SWAP)
    total = image(field) + sent.astype(F32)
    total = total.astype(BF).reshape(-1, rows, pixels)
    pieces = lax.all_to_all(total, ("y", "xh", "z"), 0, 0, tiled=True)
    image_rows = jnp.sum(pieces.astype(F32), axis=0, keepdims=True)
    return jnp.where(section == 0, image_rows, image_rows[:, ::-1])


def solution(mesh):
    fine = Mesh(mesh.devices.reshape(2, 4, 2, 2, 4, 2), ("s",) + TILE)
    in_specs = (P(TILE, "s", None, None), P(), P(), P(TILE, None, None), P())
    return jax.shard_map(
        on_device, mesh=fine, in_specs=in_specs, out_specs=P(TILE, "s", None), check_vma=False
    )
```

```python
import functools

import jax
import jax.numpy as jnp
from jax import lax
from jax.experimental import pallas as pl
from jax.experimental.pallas import tpu as pltpu
from jax.sharding import Mesh, PartitionSpec as P

ANG = 8
TILE = ("y", "xh", "xl", "z", "c")
SWAP = [(0, 1), (1, 0)]
BF = jnp.bfloat16
F32 = jnp.float32


def sources(out):
    return [(e, (e - out) // 2 + 2) for e in range(out - 4, out + 5, 2) if e >= 0]


def conv_kernel(outs, rows, pixels, block, flip_ref, *refs):
    remotes, (w_ref, h_ref, o_ref, xp) = refs[1:-4], refs[-4:]
    x_ref = refs[0]
    flip = flip_ref[0]
    taps = w_ref.shape[0]
    used = sorted({e for o in outs for e, _ in sources(o)})
    xp[:, 0:8, :] = jnp.zeros((len(used), 8, xp.shape[2]), xp.dtype)
    xp[:, pixels + 8 :, :] = jnp.zeros((len(used), 8, xp.shape[2]), xp.dtype)
    for slot, e in enumerate(used):
        if e < rows:
            row = x_ref[e + flip * (rows - 1 - 2 * e)]
        else:
            at = (e - rows) % 2
            row = remotes[(e - rows) // 2][at + flip * (1 - 2 * at)]
        xp[slot, 8 : pixels + 8, :] = row
    for i, o in enumerate(outs):
        for m in range(0, pixels, block):
            acc = jnp.zeros((block, w_ref.shape[2]), F32)
            for e, d in sources(o):
                slot = used.index(e)
                left = jnp.concatenate(
                    [xp[slot, m + 4 + 2 * j : m + 4 + 2 * j + block, :] for j in range(taps)], axis=1
                )
                acc += jnp.dot(left, w_ref[d + flip * (4 - 2 * d)], preferred_element_type=F32)
            hidden = jax.nn.gelu(acc, approximate=True).astype(BF)
            near = lax.dot_general(
                h_ref[...], hidden, (((1,), (1,)), ((), ())), preferred_element_type=F32
            )
            o_ref[i, :, m : m + block] = near.astype(BF)


def near_rows(outs, flip, features, remotes, weights, head):
    rows, pixels, channels = features.shape
    used = sorted({e for o in outs for e, _ in sources(o)})
    flops = sum(len(sources(o)) for o in outs) * 2 * pixels * weights.shape[1] * channels
    vmem = pl.BlockSpec(memory_space=pltpu.VMEM)
    return pl.pallas_call(
        functools.partial(conv_kernel, outs, rows, pixels, 256),
        out_shape=jax.ShapeDtypeStruct((len(outs), head.shape[0], pixels), BF),
        in_specs=[pl.BlockSpec(memory_space=pltpu.SMEM)] + [vmem] * (3 + len(remotes)),
        out_specs=vmem,
        scratch_shapes=[pltpu.VMEM((len(used), pixels + 16, channels), BF)],
        compiler_params=pltpu.CompilerParams(vmem_limit_bytes=24 << 20),
        cost_estimate=pl.CostEstimate(
            flops=2 * flops, bytes_accessed=4 << 20, transcendentals=len(outs) * pixels * channels
        ),
        name="near_rows",
    )(flip, features, *remotes, weights, head)


def socs_kernel(block, weight_ref, own_ref, other_ref, first_ref, second_ref, o_ref):
    half = own_ref.shape[1] // 2
    pixels = own_ref.shape[2]
    pieces = [r[k, p * half : (p + 1) * half, :] for p in (0, 1) for r in (own_ref, other_ref) for k in range(own_ref.shape[0])]
    left = jnp.concatenate(pieces, axis=0)
    rows = left.shape[0] // 2
    for n in range(0, pixels, block):
        total = jnp.zeros((rows, block), F32)
        for g_ref in (first_ref, second_ref):
            by_re = jnp.dot(left, g_ref[:, n : n + block], preferred_element_type=F32)
            by_im = jnp.dot(left, g_ref[:, pixels + n : pixels + n + block], preferred_element_type=F32)
            re = by_re[:rows] - by_im[rows:]
            im = by_im[:rows] + by_re[rows:]
            total += re * re + im * im
        o_ref[:, n : n + block] = (total * weight_ref[0]).astype(BF)


def socs_image(weight, own, other, first, second):
    groups, lines, pixels = own.shape
    rows = groups * lines
    vmem = pl.BlockSpec(memory_space=pltpu.VMEM)
    return pl.pallas_call(
        functools.partial(socs_kernel, 256),
        out_shape=jax.ShapeDtypeStruct((rows, pixels), BF),
        in_specs=[pl.BlockSpec(memory_space=pltpu.SMEM)] + [vmem] * 4,
        out_specs=vmem,
        compiler_params=pltpu.CompilerParams(vmem_limit_bytes=24 << 20),
        cost_estimate=pl.CostEstimate(
            flops=16 * rows * pixels * pixels, bytes_accessed=9 << 20, transcendentals=0
        ),
        name="socs_image",
    )(weight, own, other, first, second)


def ring(count, step):
    return [(i, (i + step) % count) for i in range(count)]


def hold(value, *others):
    return lax.optimization_barrier((value,) + others)[0]


def to_angles(near):
    pixels = near.shape[2]
    near = near.reshape(2, ANG, 2, pixels).transpose(1, 2, 0, 3)
    field = lax.all_to_all(near, ("y", "xh"), 0, 0, tiled=True)
    return field.transpose(1, 2, 0, 3).reshape(4 * ANG, pixels)


def along_z(field):
    count = lax.axis_size("z")
    return jnp.stack([field] + [lax.ppermute(field, "z", ring(count, k)) for k in range(1, count)])


def on_device(features, conv_weight, head_weight, kernels, source_weights):
    rows, pixels, channels = features.shape[1:]
    angle = lax.axis_index(("y", "xh"))
    section = lax.axis_index("s")
    weight = lax.dynamic_slice_in_dim(source_weights, angle, 1, 0)
    window = features[0]
    edge = lax.dynamic_slice_in_dim(window, (1 - section) * (rows - 2), 2, 0)
    remote1 = lax.ppermute(edge, "s", SWAP)
    remote2 = lax.ppermute(window[2:4], "s", SWAP)
    mine = kernels[0]
    sibling = lax.ppermute(mine, "c", SWAP)
    flip = section.astype(jnp.int32).reshape(1)
    taps = conv_weight.reshape(conv_weight.shape[0], -1, channels)
    head = head_weight.T
    near_a = near_rows((0, 1), flip, window, [], taps, head)
    field_a = to_angles(near_a)
    own_a = along_z(field_a)
    remote1 = hold(remote1, field_a, sibling)
    near_b = near_rows((2, 3), flip, window, [remote1], taps, head)
    field_b = to_angles(near_b)
    own_b = along_z(field_b)
    other_a = lax.ppermute(own_a, "xl", SWAP)
    remote2 = hold(remote2, field_b, own_a)
    near_c = near_rows((4, 5), flip, window, [remote1, remote2], taps, head)
    near_c = hold(near_c, own_b, other_a)
    other_b = lax.ppermute(own_b, "xl", SWAP)
    field_c = hold(to_angles(near_c), other_b)
    own_c = along_z(field_c)
    other_c = lax.ppermute(own_c, "xl", SWAP)
    fields = [(own_a, other_a), (own_b, other_b), (own_c, other_c)]
    images = [socs_image(weight, own, other, mine, sibling) for own, other in fields]
    count = lax.axis_size("z")
    image = jnp.stack(images).reshape(rows // 2, 2, count, 2, ANG, pixels)
    image = image.transpose(4, 1, 2, 0, 3, 5)
    image = jnp.where(lax.axis_index("xl") == 0, image, image[:, ::-1])
    image = image.reshape(2 * ANG, count * rows, pixels)
    pieces = lax.all_to_all(image, ("y", "xh", "xl"), 0, 0, tiled=True)
    parts = jnp.sum(pieces.astype(F32), axis=0).reshape(count, rows, pixels)
    total = parts[0]
    for k in range(1, count):
        total = total + lax.ppermute(parts[k], "z", ring(count, count - k))
    return jnp.where(section == 0, total, total[::-1])[None]


def solution(mesh):
    fine = Mesh(mesh.devices.reshape(2, 4, 2, 2, 4, 2), ("s",) + TILE)
    in_specs = (P(TILE, "s", None, None), P(), P(), P(TILE, None, None), P())
    return jax.shard_map(
        on_device, mesh=fine, in_specs=in_specs, out_specs=P(TILE, "s", None), check_vma=False
    )
```

```python
import functools

import jax
import jax.numpy as jnp
from jax import lax
from jax.experimental import pallas as pl
from jax.experimental.pallas import tpu as pltpu
from jax.sharding import Mesh, PartitionSpec as P

ANG = 8
TILE = ("y", "xh", "xl", "z", "c")
SWAP = [(0, 1), (1, 0)]
BF = jnp.bfloat16
F32 = jnp.float32
LINES = 6
OWN = 3
STAGES = (((0, 1, 2), (0,)), ((3, 4), (1, 2)), ((5,), (3, 4, 5)))


def touched(lines):
    return [o for o in range(LINES) if any(abs(i - o) <= 2 for i in lines)]


def conv_kernel(lines, done, before, pixels, block, flip_ref, *refs):
    x_ref, w_ref, h_ref = refs[:3]
    held = refs[3] if before else None
    outputs = refs[4 if before else 3 :]
    near_ref, xp = outputs[0], outputs[-1]
    later = [o for o in touched(lines) if o not in done]
    flip = flip_ref[0]
    taps = w_ref.shape[0]
    for slot, i in enumerate(lines):
        if i < OWN:
            row = x_ref[2 * i + flip * (LINES - 1 - 4 * i)]
        else:
            at = i - lines[0]
            row = x_ref[at + flip * (len(lines) - 1 - 2 * at)]
        xp[slot, 0:8, :] = jnp.zeros((8, xp.shape[2]), xp.dtype)
        xp[slot, pixels + 8 :, :] = jnp.zeros((8, xp.shape[2]), xp.dtype)
        xp[slot, 8 : pixels + 8, :] = row
    for m in range(0, pixels, block):
        lefts = [
            jnp.concatenate(
                [xp[slot, m + 4 + 2 * j : m + 4 + 2 * j + block, :] for j in range(taps)], axis=1
            )
            for slot in range(len(lines))
        ]
        for o in touched(lines):
            acc = held[before.index(o), m : m + block, :] if o in before else None
            for slot, i in enumerate(lines):
                d = i - o + 2
                if 0 <= d <= 4:
                    part = jnp.dot(
                        lefts[slot], w_ref[d + flip * (4 - 2 * d)], preferred_element_type=F32
                    )
                    acc = part if acc is None else acc + part
            if o in done:
                hidden = jax.nn.gelu(acc, approximate=True).astype(BF)
                near = lax.dot_general(
                    h_ref[...], hidden, (((1,), (1,)), ((), ())), preferred_element_type=F32
                )
                near_ref[done.index(o), :, m : m + block] = near.astype(BF)
            else:
                outputs[1][later.index(o), m : m + block, :] = acc


def conv_stage(stage, flip, rows, weights, head, held):
    lines, done = STAGES[stage]
    pixels, channels = rows.shape[1:]
    before = [o for o in touched(STAGES[stage - 1][0]) if o not in STAGES[stage - 1][1]] if stage else []
    later = [o for o in touched(lines) if o not in done]
    out_shape = [jax.ShapeDtypeStruct((len(done), head.shape[0], pixels), BF)]
    if later:
        out_shape.append(jax.ShapeDtypeStruct((len(later), pixels, channels), F32))
    terms = sum(abs(i - o) <= 2 for i in lines for o in range(LINES))
    vmem = pl.BlockSpec(memory_space=pltpu.VMEM)
    out = pl.pallas_call(
        functools.partial(conv_kernel, lines, done, before, pixels, 256),
        out_shape=out_shape,
        in_specs=[pl.BlockSpec(memory_space=pltpu.SMEM)] + [vmem] * (3 + len(held)),
        out_specs=[vmem] * len(out_shape),
        scratch_shapes=[pltpu.VMEM((len(lines), pixels + 16, channels), BF)],
        compiler_params=pltpu.CompilerParams(vmem_limit_bytes=24 << 20),
        cost_estimate=pl.CostEstimate(
            flops=4 * terms * pixels * weights.shape[1] * channels,
            bytes_accessed=4 << 20,
            transcendentals=len(done) * pixels * channels,
        ),
        name="conv_stage",
    )(flip, rows, weights, head, *held)
    return out[0], list(out[1:])


def socs_kernel(block, weight_ref, left_ref, first_ref, second_ref, o_ref):
    rows, pixels = o_ref.shape
    left = left_ref[...]
    for n in range(0, pixels, block):
        total = jnp.zeros((rows, block), F32)
        for g_ref in (first_ref, second_ref):
            by_re = jnp.dot(left, g_ref[:, n : n + block], preferred_element_type=F32)
            by_im = jnp.dot(left, g_ref[:, pixels + n : pixels + n + block], preferred_element_type=F32)
            re = by_re[:rows] - by_im[rows:]
            im = by_im[:rows] + by_re[rows:]
            total += re * re + im * im
        o_ref[:, n : n + block] = (total * weight_ref[0]).astype(BF)


def socs_image(weight, field, first, second):
    rows, pixels = field.shape[0] // 2, field.shape[1]
    vmem = pl.BlockSpec(memory_space=pltpu.VMEM)
    return pl.pallas_call(
        functools.partial(socs_kernel, 256),
        out_shape=jax.ShapeDtypeStruct((rows, pixels), BF),
        in_specs=[pl.BlockSpec(memory_space=pltpu.SMEM)] + [vmem] * 3,
        out_specs=vmem,
        compiler_params=pltpu.CompilerParams(vmem_limit_bytes=32 << 20),
        cost_estimate=pl.CostEstimate(
            flops=16 * rows * pixels * pixels, bytes_accessed=9 << 20, transcendentals=0
        ),
        name="socs_image",
    )(weight, field, first, second)


def on_device(features, conv_weight, head_weight, kernels, source_weights):
    rows, pixels, channels = features.shape[1:]
    angle = lax.axis_index(("y", "xh"))
    section = lax.axis_index("s")
    depth = lax.axis_size("z")
    weight = lax.dynamic_slice_in_dim(source_weights, angle, 1, 0)
    window = features[0]
    pairs = window.reshape(rows // 2, 2, pixels, channels)

    def halo(start, count):
        block = lax.dynamic_slice(pairs, (start, 1 - section, 0, 0), (count, 1, pixels, channels))
        return lax.ppermute(block[:, 0], "s", SWAP)

    first = halo(1 - section, 2)
    last = halo(2 * section, 1)
    mine = kernels[0]
    sibling = lax.ppermute(mine, "c", SWAP)
    flip = section.astype(jnp.int32).reshape(1)
    taps = conv_weight.reshape(conv_weight.shape[0], -1, channels)
    head = head_weight.T
    near, held = [], []
    for stage, read in enumerate((window, first, last)):
        done, held = conv_stage(stage, flip, read, taps, head, held)
        near.append(done)
    near = jnp.concatenate(near, axis=0).reshape(LINES, ANG, 2, pixels).transpose(1, 2, 0, 3)
    near = jnp.broadcast_to(near[:, None], (ANG, depth, 2, LINES, pixels))
    near = near.reshape(ANG * depth, 2, LINES, pixels)
    field = lax.all_to_all(near, ("y", "xh", "z"), 0, 0, tiled=True)
    field = field.transpose(1, 2, 0, 3).reshape(-1, pixels)
    other = lax.ppermute(field, "xl", SWAP)

    def image(part):
        part = socs_image(weight, part, mine, sibling)
        return part.reshape(LINES, ANG, depth, pixels).transpose(1, 2, 0, 3)

    own, other = image(field), image(other)
    low = lax.axis_index("xl") == 0
    images = jnp.stack([jnp.where(low, own, other), jnp.where(low, other, own)], axis=1)
    images = images.reshape(2 * ANG, depth * LINES, pixels)
    pieces = lax.all_to_all(images, ("y", "xh", "xl"), 0, 0, tiled=True)
    total = jnp.sum(pieces.astype(F32), axis=0).reshape(depth, 2, OWN, pixels)
    kept, given = total[:, 0], total[:, 1]
    stays = section == 0
    total = jnp.stack([jnp.where(stays, kept, given), jnp.where(stays, given, kept)])
    total = total.reshape(2 * depth, OWN * pixels // 128, 128)
    total = lax.all_to_all(total, ("s", "z"), 0, 0, tiled=True)
    even, odd = jnp.sum(total.reshape(2, depth, OWN, pixels), axis=1)
    return jnp.stack([even, odd[::-1]], axis=1).reshape(1, LINES, pixels)


def solution(mesh):
    fine = Mesh(mesh.devices.reshape(2, 4, 2, 2, 4, 2), ("s",) + TILE)
    in_specs = (P(TILE, "s", None, None), P(), P(), P(TILE, None, None), P())
    return jax.shard_map(
        on_device, mesh=fine, in_specs=in_specs, out_specs=P(TILE, "s", None), check_vma=False
    )
```

```python
import functools

import jax
import jax.numpy as jnp
import numpy as np
from jax import lax
from jax.experimental import pallas as pl
from jax.experimental.pallas import tpu as pltpu
from jax.sharding import Mesh, PartitionSpec as P

ANG = 8
TILE = ("y", "xh", "xl", "z", "c")
SWAP = [(0, 1), (1, 0)]
BF = jnp.bfloat16
F32 = jnp.float32
LINES = 6
OWN = 3
STAGES = (((0, 1, 2), (0,)), ((3, 4), (1, 2)), ((5,), (3, 4, 5)))


def touched(lines):
    return [o for o in range(LINES) if any(abs(i - o) <= 2 for i in lines)]


def conv_kernel(lines, done, before, pixels, block, flip_ref, *refs):
    x_ref, w_ref, h_ref = refs[:3]
    held = refs[3] if before else None
    outputs = refs[4 if before else 3 :]
    near_ref, xp = outputs[0], outputs[-1]
    later = [o for o in touched(lines) if o not in done]
    flip = flip_ref[0]
    taps = w_ref.shape[0]
    for slot, i in enumerate(lines):
        if i < OWN:
            row = x_ref[2 * i + flip * (LINES - 1 - 4 * i)]
        else:
            at = i - lines[0]
            row = x_ref[at + flip * (len(lines) - 1 - 2 * at)]
        xp[slot, 0:8, :] = jnp.zeros((8, xp.shape[2]), xp.dtype)
        xp[slot, pixels + 8 :, :] = jnp.zeros((8, xp.shape[2]), xp.dtype)
        xp[slot, 8 : pixels + 8, :] = row
    for m in range(0, pixels, block):
        lefts = [
            jnp.concatenate(
                [xp[slot, m + 4 + 2 * j : m + 4 + 2 * j + block, :] for j in range(taps)], axis=1
            )
            for slot in range(len(lines))
        ]
        for o in touched(lines):
            acc = held[before.index(o), m : m + block, :] if o in before else None
            for slot, i in enumerate(lines):
                d = i - o + 2
                if 0 <= d <= 4:
                    part = jnp.dot(
                        lefts[slot], w_ref[d + flip * (4 - 2 * d)], preferred_element_type=F32
                    )
                    acc = part if acc is None else acc + part
            if o in done:
                hidden = jax.nn.gelu(acc, approximate=True).astype(BF)
                near = lax.dot_general(
                    h_ref[...], hidden, (((1,), (1,)), ((), ())), preferred_element_type=F32
                )
                near_ref[done.index(o), :, m : m + block] = near.astype(BF)
            else:
                outputs[1][later.index(o), m : m + block, :] = acc


def conv_stage(stage, flip, rows, weights, head, held):
    lines, done = STAGES[stage]
    pixels, channels = rows.shape[1:]
    before = [o for o in touched(STAGES[stage - 1][0]) if o not in STAGES[stage - 1][1]] if stage else []
    later = [o for o in touched(lines) if o not in done]
    out_shape = [jax.ShapeDtypeStruct((len(done), head.shape[0], pixels), BF)]
    if later:
        out_shape.append(jax.ShapeDtypeStruct((len(later), pixels, channels), F32))
    terms = sum(abs(i - o) <= 2 for i in lines for o in range(LINES))
    vmem = pl.BlockSpec(memory_space=pltpu.VMEM)
    out = pl.pallas_call(
        functools.partial(conv_kernel, lines, done, before, pixels, 256),
        out_shape=out_shape,
        in_specs=[pl.BlockSpec(memory_space=pltpu.SMEM)] + [vmem] * (3 + len(held)),
        out_specs=[vmem] * len(out_shape),
        scratch_shapes=[pltpu.VMEM((len(lines), pixels + 16, channels), BF)],
        compiler_params=pltpu.CompilerParams(vmem_limit_bytes=24 << 20),
        cost_estimate=pl.CostEstimate(
            flops=4 * terms * pixels * weights.shape[1] * channels,
            bytes_accessed=4 << 20,
            transcendentals=len(done) * pixels * channels,
        ),
        name="conv_stage",
    )(flip, rows, weights, head, *held)
    return out[0], list(out[1:])


def socs_kernel(weight_ref, low_ref, order_ref, left_ref, *refs):
    re1, im1, re2, im2 = refs[:4]
    o_ref = refs[-1]
    rows = left_ref.shape[0] // 2
    left = left_ref[...]
    total = jnp.zeros((rows, re1.shape[1]), F32)
    for re_ref, im_ref in ((re1, im1), (re2, im2)):
        by_re = jnp.dot(left, re_ref[...], preferred_element_type=F32)
        by_im = jnp.dot(left, im_ref[...], preferred_element_type=F32)
        re = by_re[:rows] - by_im[rows:]
        im = by_im[:rows] + by_re[rows:]
        total += re * re + im * im
    total = jnp.dot(order_ref[...], (total * weight_ref[0]).astype(BF), preferred_element_type=F32)
    if len(refs) == 5:
        o_ref[...] = total
        return
    low = low_ref[0]
    step = rows // ANG
    for g in range(ANG):
        o_ref[g, low] = refs[4][g * step : (g + 1) * step, :].astype(BF)
        o_ref[g, 1 - low] = total[g * step : (g + 1) * step].astype(BF)


def socs_image(weight, low, order, field, first, second, own=()):
    rows, pixels = field.shape[0] // 2, field.shape[1]
    block = 256
    steps = pixels // block
    scalar = pl.BlockSpec(memory_space=pltpu.SMEM)

    def whole(array):
        return pl.BlockSpec(array.shape, lambda n: (0, 0))

    re = pl.BlockSpec((pixels, block), lambda n: (0, n))
    im = pl.BlockSpec((pixels, block), lambda n: (0, n + steps))
    image = pl.BlockSpec((rows, block), lambda n: (0, n))
    if own:
        out_shape = jax.ShapeDtypeStruct((ANG, 2, rows // ANG, pixels), BF)
        out_spec = pl.BlockSpec((ANG, 2, rows // ANG, block), lambda n: (0, 0, 0, n))
    else:
        out_shape, out_spec = jax.ShapeDtypeStruct((rows, pixels), F32), image
    return pl.pallas_call(
        socs_kernel,
        grid=(steps,),
        out_shape=out_shape,
        in_specs=[scalar, scalar, whole(order), whole(field), re, im, re, im] + [image] * len(own),
        out_specs=out_spec,
        compiler_params=pltpu.CompilerParams(vmem_limit_bytes=24 << 20),
        cost_estimate=pl.CostEstimate(
            flops=16 * rows * pixels * pixels, bytes_accessed=9 << 20, transcendentals=0
        ),
        name="socs_image",
    )(weight, low, order, field, first, first, second, second, *own)


def on_device(features, conv_weight, head_weight, kernels, source_weights):
    rows, pixels, channels = features.shape[1:]
    angle = lax.axis_index(("y", "xh"))
    section = lax.axis_index("s")
    depth = lax.axis_size("z")
    weight = lax.dynamic_slice_in_dim(source_weights, angle, 1, 0)
    window = features[0]
    pairs = window.reshape(rows // 2, 2, pixels, channels)

    def halo(start, count):
        block = lax.dynamic_slice(pairs, (start, 1 - section, 0, 0), (count, 1, pixels, channels))
        return lax.ppermute(block[:, 0], "s", SWAP)

    first = halo(1 - section, 2)
    last = halo(2 * section, 1)
    mine = kernels[0]
    sibling = lax.ppermute(lax.optimization_barrier((mine, first))[0], "c", SWAP)
    flip = section.astype(jnp.int32).reshape(1)
    taps = conv_weight.reshape(conv_weight.shape[0], -1, channels)
    head = head_weight.T
    near, held = [], []
    for stage, read in enumerate((window, first, last)):
        done, held = conv_stage(stage, flip, read, taps, head, held)
        near.append(done)
    near = jnp.concatenate(near, axis=0).reshape(LINES, ANG, 2, pixels).transpose(1, 2, 0, 3)
    near = jnp.broadcast_to(near[:, None], (ANG, depth, 2, LINES, pixels))
    near = near.reshape(ANG * depth, 2, LINES, pixels)
    field = lax.all_to_all(near, ("y", "xh", "z"), 0, 0, tiled=True)
    field = field.transpose(1, 2, 0, 3).reshape(-1, pixels)
    other = lax.ppermute(field, "xl", SWAP)

    low = lax.axis_index("xl").astype(jnp.int32).reshape(1)
    sources = ANG * depth
    order = np.eye(LINES * sources).reshape(LINES, sources, -1).transpose(1, 0, 2)
    order = jnp.asarray(order.reshape(LINES * sources, -1), BF)
    own = socs_image(weight, low, order, field, mine, sibling)
    images = socs_image(weight, low, order, other, mine, sibling, (own,))
    images = images.reshape(2 * ANG, depth * LINES, pixels)
    pieces = lax.all_to_all(images, ("y", "xh", "xl"), 0, 0, tiled=True)
    total = jnp.sum(pieces.astype(F32), axis=0).reshape(depth, 2, OWN, pixels)
    kept, given = total[:, 0], total[:, 1]
    stays = section == 0
    total = jnp.stack([jnp.where(stays, kept, given), jnp.where(stays, given, kept)])
    total = total.reshape(2 * depth, OWN * pixels // 128, 128)
    total = lax.all_to_all(total, ("s", "z"), 0, 0, tiled=True)
    even, odd = jnp.sum(total.reshape(2, depth, OWN, pixels), axis=1)
    return jnp.stack([even, odd[::-1]], axis=1).reshape(1, LINES, pixels)


def solution(mesh):
    fine = Mesh(mesh.devices.reshape(2, 4, 2, 2, 4, 2), ("s",) + TILE)
    in_specs = (P(TILE, "s", None, None), P(), P(), P(TILE, None, None), P())
    return jax.shard_map(
        on_device, mesh=fine, in_specs=in_specs, out_specs=P(TILE, "s", None), check_vma=False
    )
```

```python
import functools

import jax
import jax.numpy as jnp
import numpy as np
from jax import lax
from jax.experimental import pallas as pl
from jax.experimental.pallas import tpu as pltpu
from jax.sharding import Mesh, PartitionSpec as P

ANG = 8
TILE = ("y", "xh", "xl", "z", "c")
SWAP = [(0, 1), (1, 0)]
BF = jnp.bfloat16
F32 = jnp.float32
LINES = 6
OWN = 3
STAGES = (((0, 1, 2), (0,)), ((3, 4), (1, 2)), ((5,), (3, 4, 5)))


def touched(lines):
    return [o for o in range(LINES) if any(abs(i - o) <= 2 for i in lines)]


def conv_kernel(lines, done, before, pixels, block, flip_ref, *refs):
    x_ref, w_ref, h_ref = refs[:3]
    held = refs[3] if before else None
    outputs = refs[4 if before else 3 :]
    near_ref, xp = outputs[0], outputs[-1]
    later = [o for o in touched(lines) if o not in done]
    flip = flip_ref[0]
    taps = w_ref.shape[0]
    for slot, i in enumerate(lines):
        if i < OWN:
            row = x_ref[2 * i + flip * (LINES - 1 - 4 * i)]
        else:
            at = i - lines[0]
            row = x_ref[at + flip * (len(lines) - 1 - 2 * at)]
        xp[slot, 0:8, :] = jnp.zeros((8, xp.shape[2]), xp.dtype)
        xp[slot, pixels + 8 :, :] = jnp.zeros((8, xp.shape[2]), xp.dtype)
        xp[slot, 8 : pixels + 8, :] = row
    for m in range(0, pixels, block):
        lefts = [
            jnp.concatenate(
                [xp[slot, m + 4 + 2 * j : m + 4 + 2 * j + block, :] for j in range(taps)], axis=1
            )
            for slot in range(len(lines))
        ]
        for o in touched(lines):
            acc = held[before.index(o), m : m + block, :] if o in before else None
            for slot, i in enumerate(lines):
                d = i - o + 2
                if 0 <= d <= 4:
                    part = jnp.dot(
                        lefts[slot], w_ref[d + flip * (4 - 2 * d)], preferred_element_type=F32
                    )
                    acc = part if acc is None else acc + part
            if o in done:
                hidden = jax.nn.gelu(acc, approximate=True).astype(BF)
                near = lax.dot_general(
                    h_ref[...], hidden, (((1,), (1,)), ((), ())), preferred_element_type=F32
                )
                near_ref[done.index(o), :, m : m + block] = near.astype(BF)
            else:
                outputs[1][later.index(o), m : m + block, :] = acc


def conv_stage(stage, flip, rows, weights, head, held):
    lines, done = STAGES[stage]
    pixels, channels = rows.shape[1:]
    before = [o for o in touched(STAGES[stage - 1][0]) if o not in STAGES[stage - 1][1]] if stage else []
    later = [o for o in touched(lines) if o not in done]
    out_shape = [jax.ShapeDtypeStruct((len(done), head.shape[0], pixels), BF)]
    if later:
        out_shape.append(jax.ShapeDtypeStruct((len(later), pixels, channels), F32))
    terms = sum(abs(i - o) <= 2 for i in lines for o in range(LINES))
    vmem = pl.BlockSpec(memory_space=pltpu.VMEM)
    out = pl.pallas_call(
        functools.partial(conv_kernel, lines, done, before, pixels, 256),
        out_shape=out_shape,
        in_specs=[pl.BlockSpec(memory_space=pltpu.SMEM)] + [vmem] * (3 + len(held)),
        out_specs=[vmem] * len(out_shape),
        scratch_shapes=[pltpu.VMEM((len(lines), pixels + 16, channels), BF)],
        compiler_params=pltpu.CompilerParams(vmem_limit_bytes=24 << 20),
        cost_estimate=pl.CostEstimate(
            flops=4 * terms * pixels * weights.shape[1] * channels,
            bytes_accessed=4 << 20,
            transcendentals=len(done) * pixels * channels,
        ),
        name="conv_stage",
    )(flip, rows, weights, head, *held)
    return out[0], list(out[1:])


def socs_kernel(block, weight_ref, low_ref, order_ref, left_ref, first_ref, second_ref, *refs):
    o_ref = refs[-1]
    rows, pixels = left_ref.shape[0] // 2, left_ref.shape[1]
    step = rows // ANG
    left = left_ref[...]
    low = low_ref[0]
    for n in range(0, pixels, block):
        total = jnp.zeros((rows, block), F32)
        for g_ref in (first_ref, second_ref):
            by_re = jnp.dot(left, g_ref[:, n : n + block], preferred_element_type=F32)
            by_im = jnp.dot(left, g_ref[:, pixels + n : pixels + n + block], preferred_element_type=F32)
            re = by_re[:rows] - by_im[rows:]
            im = by_im[:rows] + by_re[rows:]
            total += re * re + im * im
        total = jnp.dot(order_ref[...], (total * weight_ref[0]).astype(BF), preferred_element_type=F32)
        if len(refs) == 1:
            o_ref[:, n : n + block] = total
        else:
            for g in range(ANG):
                held = refs[0][g * step : (g + 1) * step, n : n + block]
                o_ref[g, low, :, n : n + block] = held.astype(BF)
                o_ref[g, 1 - low, :, n : n + block] = total[g * step : (g + 1) * step].astype(BF)


def socs_image(weight, low, order, field, first, second, own=()):
    rows, pixels = field.shape[0] // 2, field.shape[1]
    scalar = pl.BlockSpec(memory_space=pltpu.SMEM)
    vmem = pl.BlockSpec(memory_space=pltpu.VMEM)
    if own:
        out_shape = jax.ShapeDtypeStruct((ANG, 2, rows // ANG, pixels), BF)
    else:
        out_shape = jax.ShapeDtypeStruct((rows, pixels), F32)
    return pl.pallas_call(
        functools.partial(socs_kernel, 256),
        out_shape=out_shape,
        in_specs=[scalar, scalar] + [vmem] * (4 + len(own)),
        out_specs=vmem,
        compiler_params=pltpu.CompilerParams(vmem_limit_bytes=16 << 20),
        cost_estimate=pl.CostEstimate(
            flops=16 * rows * pixels * pixels, bytes_accessed=9 << 20, transcendentals=0
        ),
        name="socs_image",
    )(weight, low, order, field, first, second, *own)


def resident_kernel(first_ref, second_ref, a_ref, b_ref, sems):
    copies = [
        pltpu.make_async_copy(first_ref, a_ref, sems.at[0]),
        pltpu.make_async_copy(second_ref, b_ref, sems.at[1]),
    ]
    for copy in copies:
        copy.start()
    for copy in copies:
        copy.wait()


def resident(first, second):
    return pl.pallas_call(
        resident_kernel,
        out_shape=[jax.ShapeDtypeStruct(first.shape, first.dtype)] * 2,
        in_specs=[pl.BlockSpec(memory_space=pl.ANY)] * 2,
        out_specs=[pl.BlockSpec(memory_space=pltpu.VMEM)] * 2,
        scratch_shapes=[pltpu.SemaphoreType.DMA((2,))],
        compiler_params=pltpu.CompilerParams(vmem_limit_bytes=12 << 20),
        name="resident",
    )(first, second)


def on_device(features, conv_weight, head_weight, kernels, source_weights):
    rows, pixels, channels = features.shape[1:]
    angle = lax.axis_index(("y", "xh"))
    section = lax.axis_index("s")
    depth = lax.axis_size("z")
    weight = lax.dynamic_slice_in_dim(source_weights, angle, 1, 0)
    window = features[0]
    pairs = window.reshape(rows // 2, 2, pixels, channels)

    def halo(start, count):
        block = lax.dynamic_slice(pairs, (start, 1 - section, 0, 0), (count, 1, pixels, channels))
        return lax.ppermute(block[:, 0], "s", SWAP)

    first = halo(1 - section, 2)
    last = halo(2 * section, 1)
    mine = kernels[0]
    flip = section.astype(jnp.int32).reshape(1)
    taps = conv_weight.reshape(conv_weight.shape[0], -1, channels)
    head = head_weight.T
    near, held = [], []
    for stage, read in enumerate((window, first, last)):
        done, held = conv_stage(stage, flip, read, taps, head, held)
        near.append(done)
        if stage == 2:
            sibling = lax.ppermute(lax.optimization_barrier((mine, done))[0], "c", SWAP)
    near = jnp.concatenate(near, axis=0).reshape(LINES, ANG, 2, pixels).transpose(1, 2, 0, 3)
    near = jnp.broadcast_to(near[:, None], (ANG, depth, 2, LINES, pixels))
    near = near.reshape(ANG * depth, 2, LINES, pixels)
    field = lax.all_to_all(near, ("y", "xh", "z"), 0, 0, tiled=True)
    field = field.transpose(1, 2, 0, 3).reshape(-1, pixels)
    other = lax.ppermute(field, "xl", SWAP)

    mine, sibling = resident(mine, sibling)
    low = lax.axis_index("xl").astype(jnp.int32).reshape(1)
    sources = ANG * depth
    order = np.eye(LINES * sources).reshape(LINES, sources, -1).transpose(1, 0, 2)
    order = jnp.asarray(order.reshape(LINES * sources, -1), BF)
    own = socs_image(weight, low, order, field, mine, sibling)
    images = socs_image(weight, low, order, other, mine, sibling, (own,))
    images = images.reshape(2 * ANG, depth * LINES, pixels)
    pieces = lax.all_to_all(images, ("y", "xh", "xl"), 0, 0, tiled=True)
    total = jnp.sum(pieces.astype(F32), axis=0).reshape(depth, 2, OWN, pixels)
    kept, given = total[:, 0], total[:, 1]
    stays = section == 0
    total = jnp.stack([jnp.where(stays, kept, given), jnp.where(stays, given, kept)])
    total = total.reshape(2 * depth, OWN * pixels // 128, 128)
    total = lax.all_to_all(total, ("s", "z"), 0, 0, tiled=True)
    even, odd = jnp.sum(total.reshape(2, depth, OWN, pixels), axis=1)
    return jnp.stack([even, odd[::-1]], axis=1).reshape(1, LINES, pixels)


def solution(mesh):
    fine = Mesh(mesh.devices.reshape(2, 4, 2, 2, 4, 2), ("s",) + TILE)
    in_specs = (P(TILE, "s", None, None), P(), P(), P(TILE, None, None), P())
    return jax.shard_map(
        on_device, mesh=fine, in_specs=in_specs, out_specs=P(TILE, "s", None), check_vma=False
    )
```

```python
import functools

import jax
import jax.numpy as jnp
import numpy as np
from jax import lax
from jax.experimental import pallas as pl
from jax.experimental.pallas import tpu as pltpu
from jax.sharding import Mesh, PartitionSpec as P

ANG = 8
TILE = ("y", "xh", "xl", "z", "c")
SWAP = [(0, 1), (1, 0)]
BF = jnp.bfloat16
F32 = jnp.float32
LINES = 6
OWN = 3
STAGES = (((0, 1, 2), (0,)), ((3, 4), (1, 2)), ((5,), (3, 4, 5)))


def touched(lines):
    return [o for o in range(LINES) if any(abs(i - o) <= 2 for i in lines)]


def conv_kernel(lines, done, before, pixels, block, flip_ref, *refs):
    x_ref, w_ref, h_ref = refs[:3]
    held = refs[3] if before else None
    outputs = refs[4 if before else 3 :]
    near_ref, xp = outputs[0], outputs[-1]
    later = [o for o in touched(lines) if o not in done]
    flip = flip_ref[0]
    taps = w_ref.shape[0]
    for slot, i in enumerate(lines):
        if i < OWN:
            row = x_ref[2 * i + flip * (LINES - 1 - 4 * i)]
        else:
            at = i - lines[0]
            row = x_ref[at + flip * (len(lines) - 1 - 2 * at)]
        xp[slot, 0:8, :] = jnp.zeros((8, xp.shape[2]), xp.dtype)
        xp[slot, pixels + 8 :, :] = jnp.zeros((8, xp.shape[2]), xp.dtype)
        xp[slot, 8 : pixels + 8, :] = row
    for m in range(0, pixels, block):
        lefts = [
            jnp.concatenate(
                [xp[slot, m + 4 + 2 * j : m + 4 + 2 * j + block, :] for j in range(taps)], axis=1
            )
            for slot in range(len(lines))
        ]
        for o in touched(lines):
            acc = held[before.index(o), m : m + block, :] if o in before else None
            for slot, i in enumerate(lines):
                d = i - o + 2
                if 0 <= d <= 4:
                    part = jnp.dot(
                        lefts[slot], w_ref[d + flip * (4 - 2 * d)], preferred_element_type=F32
                    )
                    acc = part if acc is None else acc + part
            if o in done:
                hidden = jax.nn.gelu(acc, approximate=True).astype(BF)
                near = lax.dot_general(
                    h_ref[...], hidden, (((1,), (1,)), ((), ())), preferred_element_type=F32
                )
                near_ref[done.index(o), :, m : m + block] = near.astype(BF)
            else:
                outputs[1][later.index(o), m : m + block, :] = acc


def conv_stage(stage, flip, rows, weights, head, held):
    lines, done = STAGES[stage]
    pixels, channels = rows.shape[1:]
    before = [o for o in touched(STAGES[stage - 1][0]) if o not in STAGES[stage - 1][1]] if stage else []
    later = [o for o in touched(lines) if o not in done]
    out_shape = [jax.ShapeDtypeStruct((len(done), head.shape[0], pixels), BF)]
    if later:
        out_shape.append(jax.ShapeDtypeStruct((len(later), pixels, channels), F32))
    terms = sum(abs(i - o) <= 2 for i in lines for o in range(LINES))
    vmem = pl.BlockSpec(memory_space=pltpu.VMEM)
    out = pl.pallas_call(
        functools.partial(conv_kernel, lines, done, before, pixels, 256),
        out_shape=out_shape,
        in_specs=[pl.BlockSpec(memory_space=pltpu.SMEM)] + [vmem] * (3 + len(held)),
        out_specs=[vmem] * len(out_shape),
        scratch_shapes=[pltpu.VMEM((len(lines), pixels + 16, channels), BF)],
        compiler_params=pltpu.CompilerParams(vmem_limit_bytes=24 << 20),
        cost_estimate=pl.CostEstimate(
            flops=4 * terms * pixels * weights.shape[1] * channels,
            bytes_accessed=4 << 20,
            transcendentals=len(done) * pixels * channels,
        ),
        name="conv_stage",
    )(flip, rows, weights, head, *held)
    return out[0], list(out[1:])


def socs_kernel(block, fields, weight_ref, low_ref, order_ref, first_ref, second_ref, *refs):
    field_refs, o_ref = refs[:fields], refs[-1]
    held = refs[fields] if len(refs) > fields + 1 else None
    count, lines, pixels = field_refs[0].shape
    half = count * lines // 2
    rows = fields * half
    left = jnp.concatenate([f[z + p] for p in (0, 1) for f in field_refs for z in range(0, count, 2)], axis=0)
    order = order_ref[...]
    step = 2 * half // ANG
    for n in range(0, pixels, block):
        cols = slice(n, n + block)
        total = jnp.zeros((rows, block), F32)
        for g_ref in (first_ref, second_ref):
            by_re = jnp.dot(left, g_ref[:, cols], preferred_element_type=F32)
            by_im = jnp.dot(left, g_ref[:, pixels + n : pixels + n + block], preferred_element_type=F32)
            re = by_re[:rows] - by_im[rows:]
            im = by_im[:rows] + by_re[rows:]
            total += re * re + im * im
        total = (total * weight_ref[0]).astype(BF)
        if held is None:
            own = jnp.dot(order, total[: 2 * half], preferred_element_type=F32)
            o_ref[: 2 * half, cols] = own.astype(BF)
            o_ref[2 * half :, cols] = total[2 * half :]
        else:
            low = low_ref[0]
            own = held[: 2 * half, cols].astype(F32)
            other = jnp.concatenate([held[2 * half :, cols], total], axis=0)
            other = jnp.dot(order, other, preferred_element_type=F32)
            for g in range(ANG):
                o_ref[g, low, :, cols] = own[g * step : (g + 1) * step].astype(BF)
                o_ref[g, 1 - low, :, cols] = other[g * step : (g + 1) * step].astype(BF)


def socs_image(weight, low, order, first, second, fields, held=()):
    count, lines, pixels = fields[0].shape
    half = count * lines // 2
    scalar = pl.BlockSpec(memory_space=pltpu.SMEM)
    vmem = pl.BlockSpec(memory_space=pltpu.VMEM)
    if held:
        out_shape = jax.ShapeDtypeStruct((ANG, 2, 2 * half // ANG, pixels), BF)
    else:
        out_shape = jax.ShapeDtypeStruct((len(fields) * half, pixels), BF)
    return pl.pallas_call(
        functools.partial(socs_kernel, 256, len(fields)),
        out_shape=out_shape,
        in_specs=[scalar, scalar] + [vmem] * (3 + len(fields) + len(held)),
        out_specs=vmem,
        compiler_params=pltpu.CompilerParams(vmem_limit_bytes=20 << 20),
        cost_estimate=pl.CostEstimate(
            flops=16 * len(fields) * half * pixels * pixels, bytes_accessed=9 << 20, transcendentals=0
        ),
        name="socs_image",
    )(weight, low, order, first, second, *fields, *held)


def resident_kernel(first_ref, second_ref, a_ref, b_ref, sems):
    copies = [
        pltpu.make_async_copy(first_ref, a_ref, sems.at[0]),
        pltpu.make_async_copy(second_ref, b_ref, sems.at[1]),
    ]
    for copy in copies:
        copy.start()
    for copy in copies:
        copy.wait()


def resident(first, second):
    return pl.pallas_call(
        resident_kernel,
        out_shape=[jax.ShapeDtypeStruct(first.shape, first.dtype)] * 2,
        in_specs=[pl.BlockSpec(memory_space=pl.ANY)] * 2,
        out_specs=[pl.BlockSpec(memory_space=pltpu.VMEM)] * 2,
        scratch_shapes=[pltpu.SemaphoreType.DMA((2,))],
        compiler_params=pltpu.CompilerParams(vmem_limit_bytes=12 << 20),
        cost_estimate=pl.CostEstimate(flops=0, bytes_accessed=4 * first.size * 2, transcendentals=0),
        name="resident",
    )(first, second)


def on_device(features, conv_weight, head_weight, kernels, source_weights):
    rows, pixels, channels = features.shape[1:]
    angle = lax.axis_index(("y", "xh"))
    section = lax.axis_index("s")
    depth = lax.axis_size("z")
    weight = lax.dynamic_slice_in_dim(source_weights, angle, 1, 0)
    window = features[0]
    pairs = window.reshape(rows // 2, 2, pixels, channels)

    def halo(start, count):
        block = lax.dynamic_slice(pairs, (start, 1 - section, 0, 0), (count, 1, pixels, channels))
        return lax.ppermute(block[:, 0], "s", SWAP)

    first = halo(1 - section, 2)
    last = halo(2 * section, 1)
    mine = kernels[0]
    flip = section.astype(jnp.int32).reshape(1)
    taps = conv_weight.reshape(conv_weight.shape[0], -1, channels)
    head = head_weight.T
    near, held = [], []
    for stage, read in enumerate((window, first, last)):
        done, held = conv_stage(stage, flip, read, taps, head, held)
        near.append(done)
        if stage == 2:
            sibling = lax.ppermute(lax.optimization_barrier((mine, done))[0], "c", SWAP)
    near = jnp.concatenate(near, axis=0).reshape(LINES, ANG, 2, pixels).transpose(1, 2, 0, 3)
    near = lax.all_to_all(near, ("y", "xh"), 0, 0, tiled=True)
    near = near.transpose(1, 2, 0, 3)
    part = LINES // 2
    own_a = lax.all_gather(near[:, :part], "z", axis=0, tiled=False)
    other_a = lax.ppermute(own_a, "xl", SWAP)
    rest = lax.optimization_barrier((near[:, part:], own_a))[0]
    own_b = lax.all_gather(rest, "z", axis=0, tiled=False)
    own_b, other_a = lax.optimization_barrier((own_b, other_a))
    other_b = lax.ppermute(own_b, "xl", SWAP)
    mine, sibling = resident(mine, sibling)
    low = lax.axis_index("xl").astype(jnp.int32).reshape(1)
    order = np.eye(ANG * depth * LINES).reshape(2, depth, part, ANG, -1).transpose(3, 1, 0, 2, 4)
    order = jnp.asarray(order.reshape(ANG * depth * LINES, -1), BF)

    def flat(block):
        return block.reshape(2 * depth, part * ANG, pixels)

    held = socs_image(weight, low, order, mine, sibling, [flat(own_a), flat(own_b), flat(other_a)])
    images = socs_image(weight, low, order, mine, sibling, [flat(other_b)], (held,))
    images = images.reshape(2 * ANG, depth * LINES, pixels)
    pieces = lax.all_to_all(images, ("y", "xh", "xl"), 0, 0, tiled=True)
    total = jnp.sum(pieces.astype(F32), axis=0).reshape(depth, 2, OWN, pixels)
    kept, given = total[:, 0], total[:, 1]
    stays = section == 0
    total = jnp.stack([jnp.where(stays, kept, given), jnp.where(stays, given, kept)])
    total = total.reshape(2 * depth, OWN * pixels // 128, 128)
    total = lax.all_to_all(total, ("s", "z"), 0, 0, tiled=True)
    even, odd = jnp.sum(total.reshape(2, depth, OWN, pixels), axis=1)
    return jnp.stack([even, odd[::-1]], axis=1).reshape(1, LINES, pixels)


def solution(mesh):
    fine = Mesh(mesh.devices.reshape(2, 4, 2, 2, 4, 2), ("s",) + TILE)
    in_specs = (P(TILE, "s", None, None), P(), P(), P(TILE, None, None), P())
    return jax.shard_map(
        on_device, mesh=fine, in_specs=in_specs, out_specs=P(TILE, "s", None), check_vma=False
    )
```

```python
import functools

import jax
import jax.numpy as jnp
import numpy as np
from jax import lax
from jax.experimental import pallas as pl
from jax.experimental.pallas import tpu as pltpu
from jax.sharding import Mesh, PartitionSpec as P

ANG = 8
TILE = ("y", "xh", "xl", "z", "c")
SWAP = [(0, 1), (1, 0)]
BF = jnp.bfloat16
F32 = jnp.float32
LINES = 6
OWN = 3
STAGES = (((0, 1, 2), (0,)), ((3, 4), (1, 2)), ((5,), (3, 4, 5)))


def touched(lines):
    return [o for o in range(LINES) if any(abs(i - o) <= 2 for i in lines)]


def conv_kernel(lines, done, before, pixels, block, flip_ref, *refs):
    x_ref, w_ref, h_ref = refs[:3]
    held = refs[3] if before else None
    outputs = refs[4 if before else 3 :]
    near_ref, xp = outputs[0], outputs[-1]
    later = [o for o in touched(lines) if o not in done]
    flip = flip_ref[0]
    taps = w_ref.shape[0]
    for slot, i in enumerate(lines):
        if i < OWN:
            row = x_ref[2 * i + flip * (LINES - 1 - 4 * i)]
        else:
            at = i - lines[0]
            row = x_ref[at + flip * (len(lines) - 1 - 2 * at)]
        xp[slot, 0:8, :] = jnp.zeros((8, xp.shape[2]), xp.dtype)
        xp[slot, pixels + 8 :, :] = jnp.zeros((8, xp.shape[2]), xp.dtype)
        xp[slot, 8 : pixels + 8, :] = row
    for m in range(0, pixels, block):
        lefts = [
            jnp.concatenate(
                [xp[slot, m + 4 + 2 * j : m + 4 + 2 * j + block, :] for j in range(taps)], axis=1
            )
            for slot in range(len(lines))
        ]
        for o in touched(lines):
            acc = held[before.index(o), m : m + block, :] if o in before else None
            for slot, i in enumerate(lines):
                d = i - o + 2
                if 0 <= d <= 4:
                    part = jnp.dot(
                        lefts[slot], w_ref[d + flip * (4 - 2 * d)], preferred_element_type=F32
                    )
                    acc = part if acc is None else acc + part
            if o in done:
                hidden = jax.nn.gelu(acc, approximate=True).astype(BF)
                near = lax.dot_general(
                    h_ref[...], hidden, (((1,), (1,)), ((), ())), preferred_element_type=F32
                )
                near_ref[done.index(o), :, m : m + block] = near.astype(BF)
            else:
                outputs[1][later.index(o), m : m + block, :] = acc


def conv_stage(stage, flip, rows, weights, head, held):
    lines, done = STAGES[stage]
    pixels, channels = rows.shape[1:]
    before = [o for o in touched(STAGES[stage - 1][0]) if o not in STAGES[stage - 1][1]] if stage else []
    later = [o for o in touched(lines) if o not in done]
    out_shape = [jax.ShapeDtypeStruct((len(done), head.shape[0], pixels), BF)]
    if later:
        out_shape.append(jax.ShapeDtypeStruct((len(later), pixels, channels), F32))
    terms = sum(abs(i - o) <= 2 for i in lines for o in range(LINES))
    vmem = pl.BlockSpec(memory_space=pltpu.VMEM)
    out = pl.pallas_call(
        functools.partial(conv_kernel, lines, done, before, pixels, 256),
        out_shape=out_shape,
        in_specs=[pl.BlockSpec(memory_space=pltpu.SMEM)] + [vmem] * (3 + len(held)),
        out_specs=[vmem] * len(out_shape),
        scratch_shapes=[pltpu.VMEM((len(lines), pixels + 16, channels), BF)],
        compiler_params=pltpu.CompilerParams(vmem_limit_bytes=24 << 20),
        cost_estimate=pl.CostEstimate(
            flops=4 * terms * pixels * weights.shape[1] * channels,
            bytes_accessed=4 << 20,
            transcendentals=len(done) * pixels * channels,
        ),
        name="conv_stage",
    )(flip, rows, weights, head, *held)
    return out[0], list(out[1:])


def socs_kernel(block, fields, weight_ref, low_ref, order_ref, first_ref, second_ref, *refs):
    field_refs, o_ref = refs[:fields], refs[-1]
    held = refs[fields] if len(refs) > fields + 1 else None
    pixels = field_refs[0].shape[2]
    left = [f[z + p] for p in (0, 1) for f in field_refs for z in range(0, f.shape[0], 2)]
    left = jnp.concatenate(left, axis=0)
    rows = left.shape[0] // 2
    order = order_ref[...]
    size = order.shape[0]
    step = size // ANG
    for n in range(0, pixels, block):
        cols = slice(n, n + block)
        total = jnp.zeros((rows, block), F32)
        for g_ref in (first_ref, second_ref):
            by_re = jnp.dot(left, g_ref[:, cols], preferred_element_type=F32)
            by_im = jnp.dot(left, g_ref[:, pixels + n : pixels + n + block], preferred_element_type=F32)
            re = by_re[:rows] - by_im[rows:]
            im = by_im[:rows] + by_re[rows:]
            total += re * re + im * im
        total = (total * weight_ref[0]).astype(BF)
        if held is None:
            own = jnp.dot(order, total[:size], preferred_element_type=F32)
            o_ref[:size, cols] = own.astype(BF)
            o_ref[size:, cols] = total[size:]
        else:
            low = low_ref[0]
            own = held[:size, cols].astype(F32)
            other = jnp.concatenate([held[size:, cols], total], axis=0)
            other = jnp.dot(order, other, preferred_element_type=F32)
            for g in range(ANG):
                o_ref[g, low, :, cols] = own[g * step : (g + 1) * step].astype(BF)
                o_ref[g, 1 - low, :, cols] = other[g * step : (g + 1) * step].astype(BF)


def socs_image(weight, low, order, first, second, fields, held=()):
    pixels = fields[0].shape[2]
    rows = sum(f.shape[0] * f.shape[1] for f in fields) // 2
    scalar = pl.BlockSpec(memory_space=pltpu.SMEM)
    vmem = pl.BlockSpec(memory_space=pltpu.VMEM)
    if held:
        out_shape = jax.ShapeDtypeStruct((ANG, 2, order.shape[0] // ANG, pixels), BF)
    else:
        out_shape = jax.ShapeDtypeStruct((rows, pixels), BF)
    return pl.pallas_call(
        functools.partial(socs_kernel, 256, len(fields)),
        out_shape=out_shape,
        in_specs=[scalar, scalar] + [vmem] * (3 + len(fields) + len(held)),
        out_specs=vmem,
        compiler_params=pltpu.CompilerParams(vmem_limit_bytes=20 << 20),
        cost_estimate=pl.CostEstimate(
            flops=16 * rows * pixels * pixels, bytes_accessed=9 << 20, transcendentals=0
        ),
        name="socs_image",
    )(weight, low, order, first, second, *fields, *held)


def resident_kernel(first_ref, second_ref, a_ref, b_ref, sems):
    copies = [
        pltpu.make_async_copy(first_ref, a_ref, sems.at[0]),
        pltpu.make_async_copy(second_ref, b_ref, sems.at[1]),
    ]
    for copy in copies:
        copy.start()
    for copy in copies:
        copy.wait()


def resident(first, second):
    return pl.pallas_call(
        resident_kernel,
        out_shape=[jax.ShapeDtypeStruct(first.shape, first.dtype)] * 2,
        in_specs=[pl.BlockSpec(memory_space=pl.ANY)] * 2,
        out_specs=[pl.BlockSpec(memory_space=pltpu.VMEM)] * 2,
        scratch_shapes=[pltpu.SemaphoreType.DMA((2,))],
        compiler_params=pltpu.CompilerParams(vmem_limit_bytes=12 << 20),
        cost_estimate=pl.CostEstimate(flops=0, bytes_accessed=4 * first.size * 2, transcendentals=0),
        name="resident",
    )(first, second)


def on_device(features, conv_weight, head_weight, kernels, source_weights):
    rows, pixels, channels = features.shape[1:]
    angle = lax.axis_index(("y", "xh"))
    section = lax.axis_index("s")
    depth = lax.axis_size("z")
    weight = lax.dynamic_slice_in_dim(source_weights, angle, 1, 0)
    window = features[0]
    pairs = window.reshape(rows // 2, 2, pixels, channels)

    def halo(start, count):
        block = lax.dynamic_slice(pairs, (start, 1 - section, 0, 0), (count, 1, pixels, channels))
        return lax.ppermute(block[:, 0], "s", SWAP)

    first = halo(1 - section, 2)
    last = halo(2 * section, 1)
    mine = kernels[0]
    flip = section.astype(jnp.int32).reshape(1)
    taps = conv_weight.reshape(conv_weight.shape[0], -1, channels)
    head = head_weight.T
    near, held = [], []
    for stage, read in enumerate((window, first, last)):
        done, held = conv_stage(stage, flip, read, taps, head, held)
        near.append(done)
        if stage == 2:
            sibling = lax.ppermute(lax.optimization_barrier((mine, done))[0], "c", SWAP)
    near = jnp.concatenate(near, axis=0).reshape(LINES, ANG, 2, pixels).transpose(1, 2, 0, 3)
    near = lax.all_to_all(near, ("y", "xh"), 0, 0, tiled=True)
    own = lax.all_gather(near.transpose(1, 2, 0, 3), "z", axis=0, tiled=False)
    own = own.reshape(2 * depth, LINES * ANG, pixels)
    other_a = lax.ppermute(own[:depth], "xl", SWAP)
    other_b = lax.ppermute(own[depth:], "xl", SWAP)
    mine, sibling = resident(mine, sibling)
    low = lax.axis_index("xl").astype(jnp.int32).reshape(1)
    order = np.eye(ANG * depth * LINES).reshape(depth, LINES, ANG, -1).transpose(2, 0, 1, 3)
    order = jnp.asarray(order.reshape(ANG * depth * LINES, -1), BF)
    held = socs_image(weight, low, order, mine, sibling, [own, other_a])
    images = socs_image(weight, low, order, mine, sibling, [other_b], (held,))
    images = images.reshape(2 * ANG, depth * LINES, pixels)
    pieces = lax.all_to_all(images, ("y", "xh", "xl"), 0, 0, tiled=True)
    total = jnp.sum(pieces.astype(F32), axis=0).reshape(depth, 2, OWN, pixels)
    kept, given = total[:, 0], total[:, 1]
    stays = section == 0
    total = jnp.stack([jnp.where(stays, kept, given), jnp.where(stays, given, kept)])
    total = total.reshape(2 * depth, OWN * pixels // 128, 128)
    total = lax.all_to_all(total, ("s", "z"), 0, 0, tiled=True)
    even, odd = jnp.sum(total.reshape(2, depth, OWN, pixels), axis=1)
    return jnp.stack([even, odd[::-1]], axis=1).reshape(1, LINES, pixels)


def solution(mesh):
    fine = Mesh(mesh.devices.reshape(2, 4, 2, 2, 4, 2), ("s",) + TILE)
    in_specs = (P(TILE, "s", None, None), P(), P(), P(TILE, None, None), P())
    return jax.shard_map(
        on_device, mesh=fine, in_specs=in_specs, out_specs=P(TILE, "s", None), check_vma=False
    )
```

```python
import functools

import jax
import jax.numpy as jnp
import numpy as np
from jax import lax
from jax.experimental import pallas as pl
from jax.experimental.pallas import tpu as pltpu
from jax.sharding import Mesh, PartitionSpec as P

ANG = 8
TILE = ("y", "xh", "xl", "z", "c")
SWAP = [(0, 1), (1, 0)]
BF = jnp.bfloat16
F32 = jnp.float32
LINES = 6
OWN = 3
STAGES = (((0, 1, 2), (0,)), ((3, 4), (1, 2)), ((5,), (3, 4, 5)))


def touched(lines):
    return [o for o in range(LINES) if any(abs(i - o) <= 2 for i in lines)]


def conv_kernel(lines, done, before, pixels, block, flip_ref, *refs):
    x_ref, w_ref, h_ref = refs[:3]
    held = refs[3] if before else None
    outputs = refs[4 if before else 3 :]
    near_ref, xp = outputs[0], outputs[-1]
    later = [o for o in touched(lines) if o not in done]
    flip = flip_ref[0]
    taps = w_ref.shape[0]
    for slot, i in enumerate(lines):
        if i < OWN:
            row = x_ref[2 * i + flip * (LINES - 1 - 4 * i)]
        else:
            at = i - lines[0]
            row = x_ref[at + flip * (len(lines) - 1 - 2 * at)]
        xp[slot, 0:8, :] = jnp.zeros((8, xp.shape[2]), xp.dtype)
        xp[slot, pixels + 8 :, :] = jnp.zeros((8, xp.shape[2]), xp.dtype)
        xp[slot, 8 : pixels + 8, :] = row
    for m in range(0, pixels, block):
        lefts = [
            jnp.concatenate(
                [xp[slot, m + 4 + 2 * j : m + 4 + 2 * j + block, :] for j in range(taps)], axis=1
            )
            for slot in range(len(lines))
        ]
        for o in touched(lines):
            acc = held[before.index(o), m : m + block, :] if o in before else None
            for slot, i in enumerate(lines):
                d = i - o + 2
                if 0 <= d <= 4:
                    part = jnp.dot(
                        lefts[slot], w_ref[d + flip * (4 - 2 * d)], preferred_element_type=F32
                    )
                    acc = part if acc is None else acc + part
            if o in done:
                hidden = jax.nn.gelu(acc, approximate=True).astype(BF)
                near = lax.dot_general(
                    h_ref[...], hidden, (((1,), (1,)), ((), ())), preferred_element_type=F32
                )
                near_ref[done.index(o), :, m : m + block] = near.astype(BF)
            else:
                outputs[1][later.index(o), m : m + block, :] = acc


def conv_stage(stage, flip, rows, weights, head, held):
    lines, done = STAGES[stage]
    pixels, channels = rows.shape[1:]
    before = [o for o in touched(STAGES[stage - 1][0]) if o not in STAGES[stage - 1][1]] if stage else []
    later = [o for o in touched(lines) if o not in done]
    out_shape = [jax.ShapeDtypeStruct((len(done), head.shape[0], pixels), BF)]
    if later:
        out_shape.append(jax.ShapeDtypeStruct((len(later), pixels, channels), F32))
    terms = sum(abs(i - o) <= 2 for i in lines for o in range(LINES))
    vmem = pl.BlockSpec(memory_space=pltpu.VMEM)
    out = pl.pallas_call(
        functools.partial(conv_kernel, lines, done, before, pixels, 256),
        out_shape=out_shape,
        in_specs=[pl.BlockSpec(memory_space=pltpu.SMEM)] + [vmem] * (3 + len(held)),
        out_specs=[vmem] * len(out_shape),
        scratch_shapes=[pltpu.VMEM((len(lines), pixels + 16, channels), BF)],
        compiler_params=pltpu.CompilerParams(vmem_limit_bytes=24 << 20),
        cost_estimate=pl.CostEstimate(
            flops=4 * terms * pixels * weights.shape[1] * channels,
            bytes_accessed=4 << 20,
            transcendentals=len(done) * pixels * channels,
        ),
        name="conv_stage",
    )(flip, rows, weights, head, *held)
    return out[0], list(out[1:])


def socs_kernel(block, fields, last, weight_ref, low_ref, order_ref, first_ref, second_ref, *refs):
    field_refs, o_ref = refs[:fields], refs[-1]
    held = refs[fields:-1]
    pixels = field_refs[0].shape[2]
    left = [f[z + p] for p in (0, 1) for f in field_refs for z in range(0, f.shape[0], 2)]
    left = jnp.concatenate(left, axis=0)
    rows = left.shape[0] // 2
    order = order_ref[...]
    size = order.shape[0]
    step = size // ANG
    for n in range(0, pixels, block):
        cols = slice(n, n + block)
        total = jnp.zeros((rows, block), F32)
        for g_ref in (first_ref, second_ref):
            by_re = jnp.dot(left, g_ref[:, cols], preferred_element_type=F32)
            by_im = jnp.dot(left, g_ref[:, pixels + n : pixels + n + block], preferred_element_type=F32)
            re = by_re[:rows] - by_im[rows:]
            im = by_im[:rows] + by_re[rows:]
            total += re * re + im * im
        total = (total * weight_ref[0]).astype(BF)
        if not last:
            if rows >= size:
                own = jnp.dot(order, total[:size], preferred_element_type=F32)
                o_ref[:size, cols] = own.astype(BF)
                o_ref[size:, cols] = total[size:]
            else:
                o_ref[:, cols] = total
        else:
            low = low_ref[0]
            own = held[0][:size, cols].astype(F32)
            other = jnp.concatenate([held[0][size:, cols], held[1][:, cols], total], axis=0)
            other = jnp.dot(order, other, preferred_element_type=F32)
            for g in range(ANG):
                o_ref[g, low, :, cols] = own[g * step : (g + 1) * step].astype(BF)
                o_ref[g, 1 - low, :, cols] = other[g * step : (g + 1) * step].astype(BF)


def socs_image(weight, low, order, first, second, fields, held=()):
    pixels = fields[0].shape[2]
    rows = sum(f.shape[0] * f.shape[1] for f in fields) // 2
    scalar = pl.BlockSpec(memory_space=pltpu.SMEM)
    vmem = pl.BlockSpec(memory_space=pltpu.VMEM)
    if held:
        out_shape = jax.ShapeDtypeStruct((ANG, 2, order.shape[0] // ANG, pixels), BF)
    else:
        out_shape = jax.ShapeDtypeStruct((rows, pixels), BF)
    return pl.pallas_call(
        functools.partial(socs_kernel, 256, len(fields), bool(held)),
        out_shape=out_shape,
        in_specs=[scalar, scalar] + [vmem] * (3 + len(fields) + len(held)),
        out_specs=vmem,
        compiler_params=pltpu.CompilerParams(vmem_limit_bytes=20 << 20),
        cost_estimate=pl.CostEstimate(
            flops=16 * rows * pixels * pixels, bytes_accessed=9 << 20, transcendentals=0
        ),
        name="socs_image",
    )(weight, low, order, first, second, *fields, *held)


def resident_kernel(first_ref, second_ref, a_ref, b_ref, sems):
    copies = [
        pltpu.make_async_copy(first_ref, a_ref, sems.at[0]),
        pltpu.make_async_copy(second_ref, b_ref, sems.at[1]),
    ]
    for copy in copies:
        copy.start()
    for copy in copies:
        copy.wait()


def resident(first, second):
    return pl.pallas_call(
        resident_kernel,
        out_shape=[jax.ShapeDtypeStruct(first.shape, first.dtype)] * 2,
        in_specs=[pl.BlockSpec(memory_space=pl.ANY)] * 2,
        out_specs=[pl.BlockSpec(memory_space=pltpu.VMEM)] * 2,
        scratch_shapes=[pltpu.SemaphoreType.DMA((2,))],
        compiler_params=pltpu.CompilerParams(vmem_limit_bytes=12 << 20),
        cost_estimate=pl.CostEstimate(flops=0, bytes_accessed=4 * first.size * 2, transcendentals=0),
        name="resident",
    )(first, second)


def on_device(features, conv_weight, head_weight, kernels, source_weights):
    rows, pixels, channels = features.shape[1:]
    angle = lax.axis_index(("y", "xh"))
    section = lax.axis_index("s")
    depth = lax.axis_size("z")
    weight = lax.dynamic_slice_in_dim(source_weights, angle, 1, 0)
    window = features[0]
    pairs = window.reshape(rows // 2, 2, pixels, channels)

    def halo(start, count):
        block = lax.dynamic_slice(pairs, (start, 1 - section, 0, 0), (count, 1, pixels, channels))
        return lax.ppermute(block[:, 0], "s", SWAP)

    first = halo(1 - section, 2)
    last = halo(2 * section, 1)
    mine = kernels[0]
    flip = section.astype(jnp.int32).reshape(1)
    taps = conv_weight.reshape(conv_weight.shape[0], -1, channels)
    head = head_weight.T
    near, held = [], []
    for stage, read in enumerate((window, first, last)):
        done, held = conv_stage(stage, flip, read, taps, head, held)
        near.append(done)
        if stage == 2:
            sibling = lax.ppermute(lax.optimization_barrier((mine, done))[0], "c", SWAP)
    near = jnp.concatenate(near, axis=0).reshape(LINES, ANG, 2, pixels).transpose(1, 2, 0, 3)
    near = lax.all_to_all(near, ("y", "xh"), 0, 0, tiled=True)
    near = near.transpose(1, 2, 0, 3).reshape(2, LINES * ANG, pixels)
    early = lax.ppermute(near, "xl", SWAP)
    own = lax.all_gather(near, "z", axis=0, tiled=True)
    own, early = lax.optimization_barrier((own, early))
    at = lax.axis_index("z")

    def ahead(k):
        return lax.dynamic_slice_in_dim(own, 2 * lax.rem(at + k, depth), 2, 0)

    other_a = lax.ppermute(jnp.concatenate([ahead(1), ahead(2)], axis=0), "xl", SWAP)
    other_b = lax.ppermute(ahead(3), "xl", SWAP)
    mine, sibling = resident(mine, sibling)
    low = lax.axis_index("xl").astype(jnp.int32).reshape(1)
    order = np.eye(ANG * depth * LINES).reshape(depth, LINES, ANG, -1).transpose(2, 0, 1, 3)
    order = order.reshape(ANG * depth * LINES, -1)
    width = LINES * ANG
    shifted = jnp.asarray(np.concatenate([order, order], axis=1).reshape(-1, 2 * depth, width).transpose(1, 0, 2), BF)
    shifted = lax.dynamic_slice_in_dim(shifted, at, depth, 0).transpose(1, 0, 2).reshape(order.shape)
    order = jnp.asarray(order, BF)
    held_a = socs_image(weight, low, order, mine, sibling, [own, early])
    held_b = socs_image(weight, low, order, mine, sibling, [other_a])
    images = socs_image(weight, low, shifted, mine, sibling, [other_b], (held_a, held_b))
    images = images.reshape(2 * ANG, depth * LINES, pixels)
    pieces = lax.all_to_all(images, ("y", "xh", "xl"), 0, 0, tiled=True)
    total = jnp.sum(pieces.astype(F32), axis=0).reshape(depth, 2, OWN, pixels)
    kept, given = total[:, 0], total[:, 1]
    stays = section == 0
    total = jnp.stack([jnp.where(stays, kept, given), jnp.where(stays, given, kept)])
    total = total.reshape(2 * depth, OWN * pixels // 128, 128)
    total = lax.all_to_all(total, ("s", "z"), 0, 0, tiled=True)
    even, odd = jnp.sum(total.reshape(2, depth, OWN, pixels), axis=1)
    return jnp.stack([even, odd[::-1]], axis=1).reshape(1, LINES, pixels)


def solution(mesh):
    fine = Mesh(mesh.devices.reshape(2, 4, 2, 2, 4, 2), ("s",) + TILE)
    in_specs = (P(TILE, "s", None, None), P(), P(), P(TILE, None, None), P())
    return jax.shard_map(
        on_device, mesh=fine, in_specs=in_specs, out_specs=P(TILE, "s", None), check_vma=False
    )
```

```python
import functools

import jax
import jax.numpy as jnp
import numpy as np
from jax import lax
from jax.experimental import pallas as pl
from jax.experimental.pallas import tpu as pltpu
from jax.sharding import Mesh, PartitionSpec as P

ANG = 8
TILE = ("y", "xh", "xl", "z", "c")
SWAP = [(0, 1), (1, 0)]
BF = jnp.bfloat16
F32 = jnp.float32
LINES = 6
OWN = 3
STAGES = (((0, 1, 2), (0,)), ((3, 4), (1, 2)), ((5,), (3, 4, 5)))


def touched(lines):
    return [o for o in range(LINES) if any(abs(i - o) <= 2 for i in lines)]


def conv_kernel(lines, done, before, pixels, block, flip_ref, *refs):
    x_ref, w_ref, h_ref = refs[:3]
    held = refs[3] if before else None
    outputs = refs[4 if before else 3 :]
    near_ref, xp = outputs[0], outputs[-1]
    later = [o for o in touched(lines) if o not in done]
    flip = flip_ref[0]
    taps = w_ref.shape[0]
    for slot, i in enumerate(lines):
        if i < OWN:
            row = x_ref[2 * i + flip * (LINES - 1 - 4 * i)]
        else:
            at = i - lines[0]
            row = x_ref[at + flip * (len(lines) - 1 - 2 * at)]
        xp[slot, 0:8, :] = jnp.zeros((8, xp.shape[2]), xp.dtype)
        xp[slot, pixels + 8 :, :] = jnp.zeros((8, xp.shape[2]), xp.dtype)
        xp[slot, 8 : pixels + 8, :] = row
    for m in range(0, pixels, block):
        lefts = [
            jnp.concatenate(
                [xp[slot, m + 4 + 2 * j : m + 4 + 2 * j + block, :] for j in range(taps)], axis=1
            )
            for slot in range(len(lines))
        ]
        for o in touched(lines):
            acc = held[before.index(o), m : m + block, :] if o in before else None
            for slot, i in enumerate(lines):
                d = i - o + 2
                if 0 <= d <= 4:
                    part = jnp.dot(
                        lefts[slot], w_ref[d + flip * (4 - 2 * d)], preferred_element_type=F32
                    )
                    acc = part if acc is None else acc + part
            if o in done:
                hidden = jax.nn.gelu(acc, approximate=True).astype(BF)
                near = lax.dot_general(
                    h_ref[...], hidden, (((1,), (1,)), ((), ())), preferred_element_type=F32
                )
                near_ref[done.index(o), :, m : m + block] = near.astype(BF)
            else:
                outputs[1][later.index(o), m : m + block, :] = acc


def conv_stage(stage, flip, rows, weights, head, held):
    lines, done = STAGES[stage]
    pixels, channels = rows.shape[1:]
    before = [o for o in touched(STAGES[stage - 1][0]) if o not in STAGES[stage - 1][1]] if stage else []
    later = [o for o in touched(lines) if o not in done]
    out_shape = [jax.ShapeDtypeStruct((len(done), head.shape[0], pixels), BF)]
    if later:
        out_shape.append(jax.ShapeDtypeStruct((len(later), pixels, channels), F32))
    terms = sum(abs(i - o) <= 2 for i in lines for o in range(LINES))
    vmem = pl.BlockSpec(memory_space=pltpu.VMEM)
    out = pl.pallas_call(
        functools.partial(conv_kernel, lines, done, before, pixels, 256),
        out_shape=out_shape,
        in_specs=[pl.BlockSpec(memory_space=pltpu.SMEM)] + [vmem] * (3 + len(held)),
        out_specs=[vmem] * len(out_shape),
        scratch_shapes=[pltpu.VMEM((len(lines), pixels + 16, channels), BF)],
        compiler_params=pltpu.CompilerParams(vmem_limit_bytes=24 << 20),
        cost_estimate=pl.CostEstimate(
            flops=4 * terms * pixels * weights.shape[1] * channels,
            bytes_accessed=4 << 20,
            transcendentals=len(done) * pixels * channels,
        ),
        name="conv_stage",
    )(flip, rows, weights, head, *held)
    return out[0], list(out[1:])


def socs_kernel(block, fields, last, weight_ref, place_ref, order_ref, first_ref, second_ref, *refs):
    field_refs, o_ref = refs[:fields], refs[-1]
    held = refs[fields:-1]
    pixels = field_refs[0].shape[2]
    left = [f[z + p] for p in (0, 1) for f in field_refs for z in range(0, f.shape[0], 2)]
    left = jnp.concatenate(left, axis=0)
    rows = left.shape[0] // 2
    order = order_ref[...]
    size = order.shape[0]
    step = size // ANG
    for n in range(0, pixels, block):
        cols = slice(n, n + block)
        total = jnp.zeros((rows, block), F32)
        for g_ref in (first_ref, second_ref):
            by_re = jnp.dot(left, g_ref[:, cols], preferred_element_type=F32)
            by_im = jnp.dot(left, g_ref[:, pixels + n : pixels + n + block], preferred_element_type=F32)
            re = by_re[:rows] - by_im[rows:]
            im = by_im[:rows] + by_re[rows:]
            total += re * re + im * im
        total = (total * weight_ref[place_ref[0]]).astype(BF)
        if not last:
            if rows >= size:
                own = jnp.dot(order, total[:size], preferred_element_type=F32)
                o_ref[:size, cols] = own.astype(BF)
                o_ref[size:, cols] = total[size:]
            else:
                o_ref[:, cols] = total
        else:
            low = place_ref[1]
            own = held[0][:size, cols].astype(F32)
            other = jnp.concatenate([held[0][size:, cols], held[1][:, cols], total], axis=0)
            other = jnp.dot(order, other, preferred_element_type=F32)
            for g in range(ANG):
                o_ref[g, low, :, cols] = own[g * step : (g + 1) * step].astype(BF)
                o_ref[g, 1 - low, :, cols] = other[g * step : (g + 1) * step].astype(BF)


def socs_image(weights, place, order, first, second, fields, held=()):
    pixels = fields[0].shape[2]
    rows = sum(f.shape[0] * f.shape[1] for f in fields) // 2
    scalar = pl.BlockSpec(memory_space=pltpu.SMEM)
    vmem = pl.BlockSpec(memory_space=pltpu.VMEM)
    if held:
        out_shape = jax.ShapeDtypeStruct((ANG, 2, order.shape[0] // ANG, pixels), BF)
    else:
        out_shape = jax.ShapeDtypeStruct((rows, pixels), BF)
    return pl.pallas_call(
        functools.partial(socs_kernel, 256, len(fields), bool(held)),
        out_shape=out_shape,
        in_specs=[scalar, scalar] + [vmem] * (3 + len(fields) + len(held)),
        out_specs=vmem,
        compiler_params=pltpu.CompilerParams(vmem_limit_bytes=20 << 20),
        cost_estimate=pl.CostEstimate(
            flops=16 * rows * pixels * pixels, bytes_accessed=9 << 20, transcendentals=0
        ),
        name="socs_image",
    )(weights, place, order, first, second, *fields, *held)


def resident_kernel(first_ref, second_ref, a_ref, b_ref, sems):
    parts = sems.shape[1]
    rows = a_ref.shape[0] // parts
    copies = [
        pltpu.make_async_copy(
            source.at[i * rows : (i + 1) * rows], target.at[i * rows : (i + 1) * rows], sems.at[k, i]
        )
        for i in range(parts)
        for k, (source, target) in enumerate(((first_ref, a_ref), (second_ref, b_ref)))
    ]
    for copy in copies:
        copy.start()
    for copy in copies:
        copy.wait()


def resident(first, second):
    return pl.pallas_call(
        resident_kernel,
        out_shape=[jax.ShapeDtypeStruct(first.shape, first.dtype)] * 2,
        in_specs=[pl.BlockSpec(memory_space=pl.ANY)] * 2,
        out_specs=[pl.BlockSpec(memory_space=pltpu.VMEM)] * 2,
        scratch_shapes=[pltpu.SemaphoreType.DMA((2, 8))],
        compiler_params=pltpu.CompilerParams(vmem_limit_bytes=12 << 20),
        cost_estimate=pl.CostEstimate(flops=0, bytes_accessed=4 * first.size * 2, transcendentals=0),
        name="resident",
    )(first, second)


def on_device(features, conv_weight, head_weight, kernels, source_weights):
    rows, pixels, channels = features.shape[1:]
    angle = lax.axis_index(("y", "xh"))
    section = lax.axis_index("s")
    depth = lax.axis_size("z")
    window = features[0]
    pairs = window.reshape(rows // 2, 2, pixels, channels)

    def halo(start, count):
        block = lax.dynamic_slice(pairs, (start, 1 - section, 0, 0), (count, 1, pixels, channels))
        return lax.ppermute(block[:, 0], "s", SWAP)

    first = halo(1 - section, 2)
    last = halo(2 * section, 1)
    mine = kernels[0]
    flip = section.astype(jnp.int32).reshape(1)
    taps = conv_weight.reshape(conv_weight.shape[0], -1, channels)
    head = head_weight.T
    near, held = [], []
    for stage, read in enumerate((window, first, last)):
        done, held = conv_stage(stage, flip, read, taps, head, held)
        near.append(done)
        if stage == 2:
            sibling = lax.ppermute(lax.optimization_barrier((mine, done))[0], "c", SWAP)
    near = jnp.concatenate(near, axis=0).reshape(LINES, ANG, 2, pixels).transpose(1, 2, 0, 3)
    near = lax.all_to_all(near, ("y", "xh"), 0, 0, tiled=True)
    near = near.transpose(1, 2, 0, 3).reshape(2, LINES * ANG, pixels)
    early = lax.ppermute(near, "xl", SWAP)
    own = lax.all_gather(near, "z", axis=0, tiled=True)
    own, early = lax.optimization_barrier((own, early))
    at = lax.axis_index("z")

    def ahead(k):
        return lax.dynamic_slice_in_dim(own, 2 * lax.rem(at + k, depth), 2, 0)

    other_a = lax.ppermute(jnp.concatenate([ahead(1), ahead(2)], axis=0), "xl", SWAP)
    other_b = lax.ppermute(ahead(3), "xl", SWAP)
    mine, sibling = resident(mine, sibling)
    place = jnp.stack([angle, lax.axis_index("xl")]).astype(jnp.int32)
    order = np.eye(ANG * depth * LINES).reshape(depth, LINES, ANG, -1).transpose(2, 0, 1, 3)
    order = order.reshape(ANG * depth * LINES, -1)
    width = LINES * ANG
    shifted = jnp.asarray(np.concatenate([order, order], axis=1).reshape(-1, 2 * depth, width).transpose(1, 0, 2), BF)
    shifted = lax.dynamic_slice_in_dim(shifted, at, depth, 0).transpose(1, 0, 2).reshape(order.shape)
    order = jnp.asarray(order, BF)
    held_a = socs_image(source_weights, place, order, mine, sibling, [own, early])
    held_b = socs_image(source_weights, place, order, mine, sibling, [other_a])
    images = socs_image(source_weights, place, shifted, mine, sibling, [other_b], (held_a, held_b))
    images = images.reshape(2 * ANG, depth * LINES, pixels)
    pieces = lax.all_to_all(images, ("y", "xh", "xl"), 0, 0, tiled=True)
    total = jnp.sum(pieces.astype(F32), axis=0).reshape(depth, 2, OWN, pixels)
    kept, given = total[:, 0], total[:, 1]
    stays = section == 0
    total = jnp.stack([jnp.where(stays, kept, given), jnp.where(stays, given, kept)])
    total = total.reshape(2 * depth, OWN * pixels // 128, 128)
    total = lax.all_to_all(total, ("s", "z"), 0, 0, tiled=True)
    even, odd = jnp.sum(total.reshape(2, depth, OWN, pixels // 128, 128), axis=1)
    return jnp.stack([even, odd[::-1]], axis=1).reshape(1, LINES, pixels)


def solution(mesh):
    fine = Mesh(mesh.devices.reshape(2, 4, 2, 2, 4, 2), ("s",) + TILE)
    in_specs = (P(TILE, "s", None, None), P(), P(), P(TILE, None, None), P())
    return jax.shard_map(
        on_device, mesh=fine, in_specs=in_specs, out_specs=P(TILE, "s", None), check_vma=False
    )
```

```python
import functools

import jax
import jax.numpy as jnp
import numpy as np
from jax import lax
from jax.experimental import pallas as pl
from jax.experimental.pallas import tpu as pltpu
from jax.sharding import Mesh, PartitionSpec as P

ANG = 8
TILE = ("y", "xh", "xl", "z", "c")
SWAP = [(0, 1), (1, 0)]
BF = jnp.bfloat16
F32 = jnp.float32
LINES = 6
OWN = 3
STAGES = (((0, 1, 2), (0,)), ((3, 4), (1, 2)), ((5,), (3, 4, 5)))


def touched(lines):
    return [o for o in range(LINES) if any(abs(i - o) <= 2 for i in lines)]


def conv_kernel(lines, done, before, pixels, block, flip_ref, *refs):
    x_ref, w_ref, h_ref = refs[:3]
    held = refs[3] if before else None
    outputs = refs[4 if before else 3 :]
    near_ref, xp = outputs[0], outputs[-1]
    later = [o for o in touched(lines) if o not in done]
    flip = flip_ref[0]
    taps = w_ref.shape[0]
    for slot, i in enumerate(lines):
        if i < OWN:
            row = x_ref[2 * i + flip * (LINES - 1 - 4 * i)]
        else:
            at = i - lines[0]
            row = x_ref[at + flip * (len(lines) - 1 - 2 * at)]
        xp[slot, 0:8, :] = jnp.zeros((8, xp.shape[2]), xp.dtype)
        xp[slot, pixels + 8 :, :] = jnp.zeros((8, xp.shape[2]), xp.dtype)
        xp[slot, 8 : pixels + 8, :] = row
    for m in range(0, pixels, block):
        lefts = [
            jnp.concatenate(
                [xp[slot, m + 4 + 2 * j : m + 4 + 2 * j + block, :] for j in range(taps)], axis=1
            )
            for slot in range(len(lines))
        ]
        for o in touched(lines):
            acc = held[before.index(o), m : m + block, :] if o in before else None
            for slot, i in enumerate(lines):
                d = i - o + 2
                if 0 <= d <= 4:
                    part = jnp.dot(
                        lefts[slot], w_ref[d + flip * (4 - 2 * d)], preferred_element_type=F32
                    )
                    acc = part if acc is None else acc + part
            if o in done:
                hidden = jax.nn.gelu(acc, approximate=True).astype(BF)
                near = lax.dot_general(
                    h_ref[...], hidden, (((1,), (1,)), ((), ())), preferred_element_type=F32
                )
                near_ref[done.index(o), :, m : m + block] = near.astype(BF)
            else:
                outputs[1][later.index(o), m : m + block, :] = acc


def conv_stage(stage, flip, rows, weights, head, held):
    lines, done = STAGES[stage]
    pixels, channels = rows.shape[1:]
    before = [o for o in touched(STAGES[stage - 1][0]) if o not in STAGES[stage - 1][1]] if stage else []
    later = [o for o in touched(lines) if o not in done]
    out_shape = [jax.ShapeDtypeStruct((len(done), head.shape[0], pixels), BF)]
    if later:
        out_shape.append(jax.ShapeDtypeStruct((len(later), pixels, channels), F32))
    terms = sum(abs(i - o) <= 2 for i in lines for o in range(LINES))
    vmem = pl.BlockSpec(memory_space=pltpu.VMEM)
    out = pl.pallas_call(
        functools.partial(conv_kernel, lines, done, before, pixels, 256),
        out_shape=out_shape,
        in_specs=[pl.BlockSpec(memory_space=pltpu.SMEM)] + [vmem] * (3 + len(held)),
        out_specs=[vmem] * len(out_shape),
        scratch_shapes=[pltpu.VMEM((len(lines), pixels + 16, channels), BF)],
        compiler_params=pltpu.CompilerParams(vmem_limit_bytes=24 << 20),
        cost_estimate=pl.CostEstimate(
            flops=4 * terms * pixels * weights.shape[1] * channels,
            bytes_accessed=4 << 20,
            transcendentals=len(done) * pixels * channels,
        ),
        name="conv_stage",
    )(flip, rows, weights, head, *held)
    return out[0], list(out[1:])


def socs_kernel(block, fields, last, weight_ref, place_ref, order_ref, first_ref, second_ref, *refs):
    field_refs, o_ref = refs[:fields], refs[-1]
    held = refs[fields:-1]
    pixels = field_refs[0].shape[2]
    left = [f[z + p] for p in (0, 1) for f in field_refs for z in range(0, f.shape[0], 2)]
    left = jnp.concatenate(left, axis=0)
    rows = left.shape[0] // 2
    order = order_ref[...]
    size = order.shape[0]
    step = size // ANG
    for n in range(0, pixels, block):
        cols = slice(n, n + block)
        total = jnp.zeros((rows, block), F32)
        for g_ref in (first_ref, second_ref):
            by_re = jnp.dot(left, g_ref[:, cols], preferred_element_type=F32)
            by_im = jnp.dot(left, g_ref[:, pixels + n : pixels + n + block], preferred_element_type=F32)
            re = by_re[:rows] - by_im[rows:]
            im = by_im[:rows] + by_re[rows:]
            total += re * re + im * im
        total = (total * weight_ref[place_ref[0]]).astype(BF)
        if not last:
            if rows >= size:
                own = jnp.dot(order, total[:size], preferred_element_type=F32)
                o_ref[:size, cols] = own.astype(BF)
                o_ref[size:, cols] = total[size:]
            else:
                o_ref[:, cols] = total
        else:
            low = place_ref[1]
            own = held[0][:size, cols].astype(F32)
            other = jnp.concatenate([held[0][size:, cols], held[1][:, cols], total], axis=0)
            other = jnp.dot(order, other, preferred_element_type=F32)
            for g in range(ANG):
                o_ref[g, low, :, cols] = own[g * step : (g + 1) * step].astype(BF)
                o_ref[g, 1 - low, :, cols] = other[g * step : (g + 1) * step].astype(BF)


def socs_image(weights, place, order, first, second, fields, held=()):
    pixels = fields[0].shape[2]
    rows = sum(f.shape[0] * f.shape[1] for f in fields) // 2
    scalar = pl.BlockSpec(memory_space=pltpu.SMEM)
    vmem = pl.BlockSpec(memory_space=pltpu.VMEM)
    if held:
        out_shape = jax.ShapeDtypeStruct((ANG, 2, order.shape[0] // ANG, pixels), BF)
    else:
        out_shape = jax.ShapeDtypeStruct((rows, pixels), BF)
    return pl.pallas_call(
        functools.partial(socs_kernel, 256, len(fields), bool(held)),
        out_shape=out_shape,
        in_specs=[scalar, scalar] + [vmem] * (3 + len(fields) + len(held)),
        out_specs=vmem,
        compiler_params=pltpu.CompilerParams(vmem_limit_bytes=20 << 20),
        cost_estimate=pl.CostEstimate(
            flops=16 * rows * pixels * pixels, bytes_accessed=9 << 20, transcendentals=0
        ),
        name="socs_image",
    )(weights, place, order, first, second, *fields, *held)


def resident_kernel(first_ref, second_ref, a_ref, b_ref, sems):
    parts = sems.shape[1]
    rows = a_ref.shape[0] // parts
    copies = [
        pltpu.make_async_copy(
            source.at[i * rows : (i + 1) * rows], target.at[i * rows : (i + 1) * rows], sems.at[k, i]
        )
        for i in range(parts)
        for k, (source, target) in enumerate(((first_ref, a_ref), (second_ref, b_ref)))
    ]
    for copy in copies:
        copy.start()
    for copy in copies:
        copy.wait()


def resident(first, second):
    return pl.pallas_call(
        resident_kernel,
        out_shape=[jax.ShapeDtypeStruct(first.shape, first.dtype)] * 2,
        in_specs=[pl.BlockSpec(memory_space=pl.ANY)] * 2,
        out_specs=[pl.BlockSpec(memory_space=pltpu.VMEM)] * 2,
        scratch_shapes=[pltpu.SemaphoreType.DMA((2, 8))],
        compiler_params=pltpu.CompilerParams(vmem_limit_bytes=12 << 20),
        cost_estimate=pl.CostEstimate(flops=0, bytes_accessed=4 * first.size * 2, transcendentals=0),
        name="resident",
    )(first, second)


def on_device(features, conv_weight, head_weight, kernels, source_weights):
    rows, pixels, channels = features.shape[1:]
    angle = lax.axis_index(("y", "xh"))
    section = lax.axis_index("s")
    depth = lax.axis_size("z")
    window = features[0]
    pairs = window.reshape(rows // 2, 2, pixels, channels)

    def halo(start, count):
        block = lax.dynamic_slice(pairs, (start, 1 - section, 0, 0), (count, 1, pixels, channels))
        return lax.ppermute(block[:, 0], "s", SWAP)

    first = halo(1 - section, 2)
    last = halo(2 * section, 1)
    mine = kernels[0]
    flip = section.astype(jnp.int32).reshape(1)
    taps = conv_weight.reshape(conv_weight.shape[0], -1, channels)
    head = head_weight.T
    near, held = [], []
    for stage, read in enumerate((window, first, last)):
        done, held = conv_stage(stage, flip, read, taps, head, held)
        near.append(done)
        if stage == 2:
            sibling = lax.ppermute(lax.optimization_barrier((mine, done))[0], "c", SWAP)
    near = jnp.concatenate(near, axis=0).reshape(LINES, ANG, 2, pixels).transpose(1, 2, 0, 3)
    at = lax.axis_index("z").astype(jnp.uint32)
    starts = [2 * ((at + k) % depth) for k in range(1, depth)]
    order = np.eye(ANG * depth * LINES).reshape(depth, LINES, ANG, -1).transpose(2, 0, 1, 3)
    order = order.reshape(ANG * depth * LINES, -1)
    width = LINES * ANG
    shifted = jnp.asarray(np.concatenate([order, order], axis=1).reshape(-1, 2 * depth, width).transpose(1, 0, 2), BF)
    shifted = lax.dynamic_slice_in_dim(shifted, at, depth, 0).transpose(1, 0, 2).reshape(order.shape)
    order = jnp.asarray(order, BF)
    place = jnp.stack([angle, lax.axis_index("xl")]).astype(jnp.int32)
    stays = section == 0
    near, starts, shifted, place, stays = lax.optimization_barrier((near, starts, shifted, place, stays))
    near = lax.all_to_all(near, ("y", "xh"), 0, 0, tiled=True)
    near = near.transpose(1, 2, 0, 3).reshape(2, LINES * ANG, pixels)
    early = lax.ppermute(near, "xl", SWAP)
    own = lax.all_gather(near, "z", axis=0, tiled=True)
    own, early = lax.optimization_barrier((own, early))
    ahead = [lax.dynamic_slice_in_dim(own, start, 2, 0) for start in starts]
    other_a = lax.ppermute(jnp.concatenate(ahead[:2], axis=0), "xl", SWAP)
    other_b = lax.ppermute(ahead[2], "xl", SWAP)
    mine, sibling = resident(mine, sibling)
    held_a = socs_image(source_weights, place, order, mine, sibling, [own, early])
    held_b = socs_image(source_weights, place, order, mine, sibling, [other_a])
    images = socs_image(source_weights, place, shifted, mine, sibling, [other_b], (held_a, held_b))
    images = images.reshape(2 * ANG, depth * LINES, pixels)
    pieces = lax.all_to_all(images, ("y", "xh", "xl"), 0, 0, tiled=True)
    total = jnp.sum(pieces.astype(F32), axis=0).reshape(depth, 2, OWN, pixels)
    kept, given = total[:, 0], total[:, 1]
    total = jnp.stack([jnp.where(stays, kept, given), jnp.where(stays, given, kept)])
    total = total.reshape(2 * depth, OWN * pixels // 128, 128)
    total = lax.all_to_all(total, ("s", "z"), 0, 0, tiled=True)
    even, odd = jnp.sum(total.reshape(2, depth, OWN, pixels // 128, 128), axis=1)
    return jnp.stack([even, odd[::-1]], axis=1).reshape(1, LINES, pixels)


def solution(mesh):
    fine = Mesh(mesh.devices.reshape(2, 4, 2, 2, 4, 2), ("s",) + TILE)
    in_specs = (P(TILE, "s", None, None), P(), P(), P(TILE, None, None), P())
    return jax.shard_map(
        on_device, mesh=fine, in_specs=in_specs, out_specs=P(TILE, "s", None), check_vma=False
    )
```

```python
import functools
import math

import jax
import jax.numpy as jnp
import numpy as np
from jax import lax
from jax.experimental import pallas as pl
from jax.experimental.pallas import tpu as pltpu
from jax.sharding import Mesh, PartitionSpec as P

ANG = 8
TILE = ("y", "xh", "xl", "z", "c")
SWAP = [(0, 1), (1, 0)]
BF = jnp.bfloat16
F32 = jnp.float32
LINES = 6
OWN = 3
STAGES = (((0, 1, 2), (0,)), ((3, 4), (1, 2)), ((5,), (3, 4, 5)))


def touched(lines):
    return [o for o in range(LINES) if any(abs(i - o) <= 2 for i in lines)]


def conv_kernel(lines, done, before, pixels, block, flip_ref, *refs):
    x_ref, w_ref, h_ref = refs[:3]
    held = refs[3] if before else None
    outputs = refs[4 if before else 3 :]
    near_ref, xp = outputs[0], outputs[-1]
    later = [o for o in touched(lines) if o not in done]
    flip = flip_ref[0]
    taps = w_ref.shape[0]
    for slot, i in enumerate(lines):
        if i < OWN:
            row = x_ref[2 * i + flip * (LINES - 1 - 4 * i)]
        else:
            at = i - lines[0]
            row = x_ref[at + flip * (len(lines) - 1 - 2 * at)]
        xp[slot, 0:8, :] = jnp.zeros((8, xp.shape[2]), xp.dtype)
        xp[slot, pixels + 8 :, :] = jnp.zeros((8, xp.shape[2]), xp.dtype)
        xp[slot, 8 : pixels + 8, :] = row
    for m in range(0, pixels, block):
        lefts = [
            jnp.concatenate(
                [xp[slot, m + 4 + 2 * j : m + 4 + 2 * j + block, :] for j in range(taps)], axis=1
            )
            for slot in range(len(lines))
        ]
        for o in touched(lines):
            acc = held[before.index(o), m : m + block, :] if o in before else None
            for slot, i in enumerate(lines):
                d = i - o + 2
                if 0 <= d <= 4:
                    part = jnp.dot(
                        lefts[slot], w_ref[d + flip * (4 - 2 * d)], preferred_element_type=F32
                    )
                    acc = part if acc is None else acc + part
            if o in done:
                scale = math.sqrt(2 / math.pi)
                curve = jnp.tanh(acc * (scale + (0.044715 * scale) * (acc * acc)))
                hidden = (0.5 * acc + 0.5 * acc * curve).astype(BF)
                near = lax.dot_general(
                    h_ref[...], hidden, (((1,), (1,)), ((), ())), preferred_element_type=F32
                )
                near_ref[done.index(o), :, m : m + block] = near.astype(BF)
            else:
                outputs[1][later.index(o), m : m + block, :] = acc


def conv_stage(stage, flip, rows, weights, head, held):
    lines, done = STAGES[stage]
    pixels, channels = rows.shape[1:]
    before = [o for o in touched(STAGES[stage - 1][0]) if o not in STAGES[stage - 1][1]] if stage else []
    later = [o for o in touched(lines) if o not in done]
    out_shape = [jax.ShapeDtypeStruct((len(done), head.shape[0], pixels), BF)]
    if later:
        out_shape.append(jax.ShapeDtypeStruct((len(later), pixels, channels), F32))
    terms = sum(abs(i - o) <= 2 for i in lines for o in range(LINES))
    vmem = pl.BlockSpec(memory_space=pltpu.VMEM)
    out = pl.pallas_call(
        functools.partial(conv_kernel, lines, done, before, pixels, 256),
        out_shape=out_shape,
        in_specs=[pl.BlockSpec(memory_space=pltpu.SMEM)] + [vmem] * (3 + len(held)),
        out_specs=[vmem] * len(out_shape),
        scratch_shapes=[pltpu.VMEM((len(lines), pixels + 16, channels), BF)],
        compiler_params=pltpu.CompilerParams(vmem_limit_bytes=24 << 20),
        cost_estimate=pl.CostEstimate(
            flops=4 * terms * pixels * weights.shape[1] * channels,
            bytes_accessed=4 << 20,
            transcendentals=len(done) * pixels * channels,
        ),
        name="conv_stage",
    )(flip, rows, weights, head, *held)
    return out[0], list(out[1:])


def socs_kernel(block, fields, last, weight_ref, place_ref, order_ref, first_ref, second_ref, *refs):
    field_refs, o_ref = refs[:fields], refs[-1]
    held = refs[fields:-1]
    pixels = field_refs[0].shape[2]
    left = [f[z + p] for p in (0, 1) for f in field_refs for z in range(0, f.shape[0], 2)]
    left = jnp.concatenate(left, axis=0)
    rows = left.shape[0] // 2
    order = order_ref[...]
    size = order.shape[0]
    step = size // ANG
    for n in range(0, pixels, block):
        cols = slice(n, n + block)
        total = jnp.zeros((rows, block), F32)
        for g_ref in (first_ref, second_ref):
            by_re = jnp.dot(left, g_ref[:, cols], preferred_element_type=F32)
            by_im = jnp.dot(left, g_ref[:, pixels + n : pixels + n + block], preferred_element_type=F32)
            re = by_re[:rows] - by_im[rows:]
            im = by_im[:rows] + by_re[rows:]
            total += re * re + im * im
        total = (total * weight_ref[place_ref[0]]).astype(BF)
        if not last:
            if rows >= size:
                own = jnp.dot(order, total[:size], preferred_element_type=F32)
                o_ref[:size, cols] = own.astype(BF)
                o_ref[size:, cols] = total[size:]
            else:
                o_ref[:, cols] = total
        else:
            low = place_ref[1]
            own = held[0][:size, cols].astype(F32)
            other = jnp.concatenate([held[0][size:, cols], held[1][:, cols], total], axis=0)
            other = jnp.dot(order, other, preferred_element_type=F32)
            for g in range(ANG):
                o_ref[g, low, :, cols] = own[g * step : (g + 1) * step].astype(BF)
                o_ref[g, 1 - low, :, cols] = other[g * step : (g + 1) * step].astype(BF)


def socs_image(weights, place, order, first, second, fields, held=()):
    pixels = fields[0].shape[2]
    rows = sum(f.shape[0] * f.shape[1] for f in fields) // 2
    scalar = pl.BlockSpec(memory_space=pltpu.SMEM)
    vmem = pl.BlockSpec(memory_space=pltpu.VMEM)
    if held:
        out_shape = jax.ShapeDtypeStruct((ANG, 2, order.shape[0] // ANG, pixels), BF)
    else:
        out_shape = jax.ShapeDtypeStruct((rows, pixels), BF)
    return pl.pallas_call(
        functools.partial(socs_kernel, 256, len(fields), bool(held)),
        out_shape=out_shape,
        in_specs=[scalar, scalar] + [vmem] * (3 + len(fields) + len(held)),
        out_specs=vmem,
        compiler_params=pltpu.CompilerParams(vmem_limit_bytes=20 << 20),
        cost_estimate=pl.CostEstimate(
            flops=16 * rows * pixels * pixels, bytes_accessed=9 << 20, transcendentals=0
        ),
        name="socs_image",
    )(weights, place, order, first, second, *fields, *held)


def resident_kernel(first_ref, second_ref, a_ref, b_ref, sems):
    parts = sems.shape[1]
    rows = a_ref.shape[0] // parts
    copies = [
        pltpu.make_async_copy(
            source.at[i * rows : (i + 1) * rows], target.at[i * rows : (i + 1) * rows], sems.at[k, i]
        )
        for i in range(parts)
        for k, (source, target) in enumerate(((first_ref, a_ref), (second_ref, b_ref)))
    ]
    for copy in copies:
        copy.start()
    for copy in copies:
        copy.wait()


def resident(first, second):
    return pl.pallas_call(
        resident_kernel,
        out_shape=[jax.ShapeDtypeStruct(first.shape, first.dtype)] * 2,
        in_specs=[pl.BlockSpec(memory_space=pl.ANY)] * 2,
        out_specs=[pl.BlockSpec(memory_space=pltpu.VMEM)] * 2,
        scratch_shapes=[pltpu.SemaphoreType.DMA((2, 8))],
        compiler_params=pltpu.CompilerParams(vmem_limit_bytes=12 << 20),
        cost_estimate=pl.CostEstimate(flops=0, bytes_accessed=4 * first.size * 2, transcendentals=0),
        name="resident",
    )(first, second)


def on_device(features, conv_weight, head_weight, kernels, source_weights):
    rows, pixels, channels = features.shape[1:]
    angle = lax.axis_index(("y", "xh"))
    section = lax.axis_index("s")
    depth = lax.axis_size("z")
    window = features[0]
    pairs = window.reshape(rows // 2, 2, pixels, channels)

    def halo(start, count):
        block = lax.dynamic_slice(pairs, (start, 1 - section, 0, 0), (count, 1, pixels, channels))
        return lax.ppermute(block[:, 0], "s", SWAP)

    first = halo(1 - section, 2)
    last = halo(2 * section, 1)
    mine = kernels[0]
    flip = section.astype(jnp.int32).reshape(1)
    taps = conv_weight.reshape(conv_weight.shape[0], -1, channels)
    head = head_weight.T
    near, held = [], []
    for stage, read in enumerate((window, first, last)):
        done, held = conv_stage(stage, flip, read, taps, head, held)
        near.append(done)
        if stage == 2:
            sibling = lax.ppermute(lax.optimization_barrier((mine, done))[0], "c", SWAP)
    near = jnp.concatenate(near, axis=0).reshape(LINES, ANG, 2, pixels).transpose(1, 2, 0, 3)
    at = lax.axis_index("z").astype(jnp.uint32)
    starts = [2 * ((at + k) % depth) for k in range(1, depth)]
    order = np.eye(ANG * depth * LINES).reshape(depth, LINES, ANG, -1).transpose(2, 0, 1, 3)
    order = order.reshape(ANG * depth * LINES, -1)
    width = LINES * ANG
    shifted = jnp.asarray(np.concatenate([order, order], axis=1).reshape(-1, 2 * depth, width).transpose(1, 0, 2), BF)
    shifted = lax.dynamic_slice_in_dim(shifted, at, depth, 0).transpose(1, 0, 2).reshape(order.shape)
    order = jnp.asarray(order, BF)
    place = jnp.stack([angle, lax.axis_index("xl")]).astype(jnp.int32)
    stays = section == 0
    near, starts, shifted, place, stays = lax.optimization_barrier((near, starts, shifted, place, stays))
    near = lax.all_to_all(near, ("y", "xh"), 0, 0, tiled=True)
    near = near.transpose(1, 2, 0, 3).reshape(2, LINES * ANG, pixels)
    early = lax.ppermute(near, "xl", SWAP)
    own = lax.all_gather(near, "z", axis=0, tiled=True)
    own, early = lax.optimization_barrier((own, early))
    ahead = [lax.dynamic_slice_in_dim(own, start, 2, 0) for start in starts]
    other_a = lax.ppermute(jnp.concatenate(ahead[:2], axis=0), "xl", SWAP)
    other_b = lax.ppermute(ahead[2], "xl", SWAP)
    mine, sibling = resident(mine, sibling)
    held_a = socs_image(source_weights, place, order, mine, sibling, [own, early])
    held_b = socs_image(source_weights, place, order, mine, sibling, [other_a])
    images = socs_image(source_weights, place, shifted, mine, sibling, [other_b], (held_a, held_b))
    images = images.reshape(2 * ANG, depth * LINES, pixels)
    pieces = lax.all_to_all(images, ("y", "xh", "xl"), 0, 0, tiled=True)
    total = jnp.sum(pieces.astype(F32), axis=0).reshape(depth, 2, OWN, pixels)
    kept, given = total[:, 0], total[:, 1]
    total = jnp.stack([jnp.where(stays, kept, given), jnp.where(stays, given, kept)], axis=1)
    total = total.reshape(2 * depth, OWN * pixels // 128, 128)
    total = lax.all_to_all(total, ("z", "s"), 0, 0, tiled=True)
    even, odd = jnp.sum(total.reshape(depth, 2, OWN, pixels // 128, 128), axis=0)
    return jnp.stack([even, odd[::-1]], axis=1).reshape(1, LINES, pixels)


def solution(mesh):
    fine = Mesh(mesh.devices.reshape(2, 4, 2, 2, 4, 2), ("s",) + TILE)
    in_specs = (P(TILE, "s", None, None), P(), P(), P(TILE, None, None), P())
    return jax.shard_map(
        on_device, mesh=fine, in_specs=in_specs, out_specs=P(TILE, "s", None), check_vma=False
    )
```

```python
import functools

import jax
import jax.numpy as jnp
import numpy as np
from jax import lax
from jax.experimental import pallas as pl
from jax.experimental.pallas import tpu as pltpu
from jax.sharding import Mesh, PartitionSpec as P

ANG = 8
TILE = ("y", "xh", "xl", "z", "c")
SWAP = [(0, 1), (1, 0)]
BF = jnp.bfloat16
F32 = jnp.float32
LINES = 6
OWN = 3
STAGES = (((0, 1, 2), (0,)), ((3, 4), (1, 2)), ((5,), (3, 4, 5)))


def touched(lines):
    return [o for o in range(LINES) if any(abs(i - o) <= 2 for i in lines)]


def conv_kernel(lines, done, before, pixels, block, flip_ref, *refs):
    x_ref, w_ref, h_ref = refs[:3]
    held = refs[3] if before else None
    outputs = refs[4 if before else 3 :]
    near_ref, xp = outputs[0], outputs[-1]
    later = [o for o in touched(lines) if o not in done]
    flip = flip_ref[0]
    taps = w_ref.shape[0]
    for slot, i in enumerate(lines):
        if i < OWN:
            row = x_ref[2 * i + flip * (LINES - 1 - 4 * i)]
        else:
            at = i - lines[0]
            row = x_ref[at + flip * (len(lines) - 1 - 2 * at)]
        xp[slot, 0:8, :] = jnp.zeros((8, xp.shape[2]), xp.dtype)
        xp[slot, pixels + 8 :, :] = jnp.zeros((8, xp.shape[2]), xp.dtype)
        xp[slot, 8 : pixels + 8, :] = row
    for m in range(0, pixels, block):
        lefts = [
            jnp.concatenate(
                [xp[slot, m + 4 + 2 * j : m + 4 + 2 * j + block, :] for j in range(taps)], axis=1
            )
            for slot in range(len(lines))
        ]
        for o in touched(lines):
            acc = held[before.index(o), m : m + block, :] if o in before else None
            for slot, i in enumerate(lines):
                d = i - o + 2
                if 0 <= d <= 4:
                    part = jnp.dot(
                        lefts[slot], w_ref[d + flip * (4 - 2 * d)], preferred_element_type=F32
                    )
                    acc = part if acc is None else acc + part
            if o in done:
                hidden = jax.nn.gelu(acc, approximate=True).astype(BF)
                near = lax.dot_general(
                    h_ref[...], hidden, (((1,), (1,)), ((), ())), preferred_element_type=F32
                )
                near_ref[done.index(o), :, m : m + block] = near.astype(BF)
            else:
                outputs[1][later.index(o), m : m + block, :] = acc


def conv_stage(stage, flip, rows, weights, head, held):
    lines, done = STAGES[stage]
    pixels, channels = rows.shape[1:]
    before = [o for o in touched(STAGES[stage - 1][0]) if o not in STAGES[stage - 1][1]] if stage else []
    later = [o for o in touched(lines) if o not in done]
    out_shape = [jax.ShapeDtypeStruct((len(done), head.shape[0], pixels), BF)]
    if later:
        out_shape.append(jax.ShapeDtypeStruct((len(later), pixels, channels), F32))
    terms = sum(abs(i - o) <= 2 for i in lines for o in range(LINES))
    vmem = pl.BlockSpec(memory_space=pltpu.VMEM)
    out = pl.pallas_call(
        functools.partial(conv_kernel, lines, done, before, pixels, pixels),
        out_shape=out_shape,
        in_specs=[pl.BlockSpec(memory_space=pltpu.SMEM)] + [vmem] * (3 + len(held)),
        out_specs=[vmem] * len(out_shape),
        scratch_shapes=[pltpu.VMEM((len(lines), pixels + 16, channels), BF)],
        compiler_params=pltpu.CompilerParams(vmem_limit_bytes=24 << 20),
        cost_estimate=pl.CostEstimate(
            flops=4 * terms * pixels * weights.shape[1] * channels,
            bytes_accessed=4 << 20,
            transcendentals=len(done) * pixels * channels,
        ),
        name="conv_stage",
    )(flip, rows, weights, head, *held)
    return out[0], list(out[1:])


def socs_kernel(block, fields, last, weight_ref, place_ref, order_ref, first_ref, second_ref, *refs):
    field_refs, o_ref = refs[:fields], refs[-1]
    held = refs[fields:-1]
    pixels = field_refs[0].shape[2]
    left = [f[z + p] for p in (0, 1) for f in field_refs for z in range(0, f.shape[0], 2)]
    left = jnp.concatenate(left, axis=0)
    rows = left.shape[0] // 2
    order = order_ref[...]
    size = order.shape[0]
    step = size // ANG
    for n in range(0, pixels, block):
        cols = slice(n, n + block)
        total = jnp.zeros((rows, block), F32)
        for g_ref in (first_ref, second_ref):
            by_re = jnp.dot(left, g_ref[:, cols], preferred_element_type=F32)
            by_im = jnp.dot(left, g_ref[:, pixels + n : pixels + n + block], preferred_element_type=F32)
            re = by_re[:rows] - by_im[rows:]
            im = by_im[:rows] + by_re[rows:]
            total += re * re + im * im
        total = (total * weight_ref[place_ref[0]]).astype(BF)
        if not last:
            if rows >= size:
                own = jnp.dot(order, total[:size], preferred_element_type=F32)
                o_ref[:size, cols] = own.astype(BF)
                o_ref[size:, cols] = total[size:]
            else:
                o_ref[:, cols] = total
        else:
            low = place_ref[1]
            own = held[0][:size, cols].astype(F32)
            other = jnp.concatenate([held[0][size:, cols], held[1][:, cols], total], axis=0)
            other = jnp.dot(order, other, preferred_element_type=F32)
            for g in range(ANG):
                o_ref[g, low, :, cols] = own[g * step : (g + 1) * step].astype(BF)
                o_ref[g, 1 - low, :, cols] = other[g * step : (g + 1) * step].astype(BF)


def socs_image(weights, place, order, first, second, fields, held=()):
    pixels = fields[0].shape[2]
    rows = sum(f.shape[0] * f.shape[1] for f in fields) // 2
    scalar = pl.BlockSpec(memory_space=pltpu.SMEM)
    vmem = pl.BlockSpec(memory_space=pltpu.VMEM)
    if held:
        out_shape = jax.ShapeDtypeStruct((ANG, 2, order.shape[0] // ANG, pixels), BF)
    else:
        out_shape = jax.ShapeDtypeStruct((rows, pixels), BF)
    return pl.pallas_call(
        functools.partial(socs_kernel, 256, len(fields), bool(held)),
        out_shape=out_shape,
        in_specs=[scalar, scalar] + [vmem] * (3 + len(fields) + len(held)),
        out_specs=vmem,
        compiler_params=pltpu.CompilerParams(vmem_limit_bytes=20 << 20),
        cost_estimate=pl.CostEstimate(
            flops=16 * rows * pixels * pixels, bytes_accessed=9 << 20, transcendentals=0
        ),
        name="socs_image",
    )(weights, place, order, first, second, *fields, *held)


def resident_kernel(first_ref, second_ref, a_ref, b_ref, sems):
    parts = sems.shape[1]
    rows = a_ref.shape[0] // parts
    copies = [
        pltpu.make_async_copy(
            source.at[i * rows : (i + 1) * rows], target.at[i * rows : (i + 1) * rows], sems.at[k, i]
        )
        for i in range(parts)
        for k, (source, target) in enumerate(((first_ref, a_ref), (second_ref, b_ref)))
    ]
    for copy in copies:
        copy.start()
    for copy in copies:
        copy.wait()


def resident(first, second):
    return pl.pallas_call(
        resident_kernel,
        out_shape=[jax.ShapeDtypeStruct(first.shape, first.dtype)] * 2,
        in_specs=[pl.BlockSpec(memory_space=pl.ANY)] * 2,
        out_specs=[pl.BlockSpec(memory_space=pltpu.VMEM)] * 2,
        scratch_shapes=[pltpu.SemaphoreType.DMA((2, 8))],
        compiler_params=pltpu.CompilerParams(vmem_limit_bytes=12 << 20),
        cost_estimate=pl.CostEstimate(flops=0, bytes_accessed=4 * first.size * 2, transcendentals=0),
        name="resident",
    )(first, second)


def on_device(features, conv_weight, head_weight, kernels, source_weights):
    rows, pixels, channels = features.shape[1:]
    angle = lax.axis_index(("y", "xh"))
    section = lax.axis_index("s")
    depth = lax.axis_size("z")
    window = features[0]
    pairs = window.reshape(rows // 2, 2, pixels, channels)

    def halo(start, count):
        block = lax.dynamic_slice(pairs, (start, 1 - section, 0, 0), (count, 1, pixels, channels))
        return lax.ppermute(block[:, 0], "s", SWAP)

    first = halo(1 - section, 2)
    last = halo(2 * section, 1)
    mine = kernels[0]
    flip = section.astype(jnp.int32).reshape(1)
    taps = conv_weight.reshape(conv_weight.shape[0], -1, channels)
    head = head_weight.T
    near, held = [], []
    for stage, read in enumerate((window, first, last)):
        done, held = conv_stage(stage, flip, read, taps, head, held)
        near.append(done)
        if stage == 2:
            sibling = lax.ppermute(lax.optimization_barrier((mine, done))[0], "c", SWAP)
    near = jnp.concatenate(near, axis=0).reshape(LINES, ANG, 2, pixels).transpose(1, 2, 0, 3)
    at = lax.axis_index("z").astype(jnp.uint32)
    starts = [2 * ((at + k) % depth) for k in range(1, depth)]
    order = np.eye(ANG * depth * LINES).reshape(depth, LINES, ANG, -1).transpose(2, 0, 1, 3)
    order = order.reshape(ANG * depth * LINES, -1)
    width = LINES * ANG
    shifted = jnp.asarray(np.concatenate([order, order], axis=1).reshape(-1, 2 * depth, width).transpose(1, 0, 2), BF)
    shifted = lax.dynamic_slice_in_dim(shifted, at, depth, 0).transpose(1, 0, 2).reshape(order.shape)
    order = jnp.asarray(order, BF)
    place = jnp.stack([angle, lax.axis_index("xl")]).astype(jnp.int32)
    stays = section == 0
    near, starts, shifted, place, stays = lax.optimization_barrier((near, starts, shifted, place, stays))
    near = lax.all_to_all(near, ("y", "xh"), 0, 0, tiled=True)
    near = near.transpose(1, 2, 0, 3).reshape(2, LINES * ANG, pixels)
    early = lax.ppermute(near, "xl", SWAP)
    own = lax.all_gather(near, "z", axis=0, tiled=True)
    own, early = lax.optimization_barrier((own, early))
    ahead = [lax.dynamic_slice_in_dim(own, start, 2, 0) for start in starts]
    other_a = lax.ppermute(jnp.concatenate(ahead[:2], axis=0), "xl", SWAP)
    other_b = lax.ppermute(ahead[2], "xl", SWAP)
    mine, sibling = resident(mine, sibling)
    held_a = socs_image(source_weights, place, order, mine, sibling, [own, early])
    held_b = socs_image(source_weights, place, order, mine, sibling, [other_a])
    images = socs_image(source_weights, place, shifted, mine, sibling, [other_b], (held_a, held_b))
    images = images.reshape(2 * ANG, depth * LINES, pixels)
    pieces = lax.all_to_all(images, ("y", "xh", "xl"), 0, 0, tiled=True)
    total = jnp.sum(pieces.astype(F32), axis=0).reshape(depth, 2, OWN, pixels)
    kept, given = total[:, 0], total[:, 1]
    total = jnp.stack([jnp.where(stays, kept, given), jnp.where(stays, given, kept)])
    total = total.reshape(2 * depth, OWN * pixels // 128, 128)
    total = lax.all_to_all(total, ("s", "z"), 0, 0, tiled=True)
    even, odd = jnp.sum(total.reshape(2, depth, OWN, pixels // 128, 128), axis=1)
    return jnp.stack([even, odd[::-1]], axis=1).reshape(1, LINES, pixels)


def solution(mesh):
    fine = Mesh(mesh.devices.reshape(2, 4, 2, 2, 4, 2), ("s",) + TILE)
    in_specs = (P(TILE, "s", None, None), P(), P(), P(TILE, None, None), P())
    return jax.shard_map(
        on_device, mesh=fine, in_specs=in_specs, out_specs=P(TILE, "s", None), check_vma=False
    )
```

```python
import functools

import jax
import jax.numpy as jnp
import numpy as np
from jax import lax
from jax.experimental import pallas as pl
from jax.experimental.pallas import tpu as pltpu
from jax.sharding import Mesh, PartitionSpec as P

ANG = 8
TILE = ("y", "xh", "xl", "z", "c")
SWAP = [(0, 1), (1, 0)]
BF = jnp.bfloat16
F32 = jnp.float32
LINES = 6
OWN = 3
STAGES = (((0, 1, 2), (0,)), ((3, 4), (1, 2)), ((5,), (3, 4, 5)))


def touched(lines):
    return [o for o in range(LINES) if any(abs(i - o) <= 2 for i in lines)]


def conv_kernel(lines, done, before, pixels, block, flip_ref, *refs):
    x_ref, w_ref, h_ref = refs[:3]
    held = refs[3] if before else None
    outputs = refs[4 if before else 3 :]
    near_ref, xp = outputs[0], outputs[-1]
    later = [o for o in touched(lines) if o not in done]
    flip = flip_ref[0]
    taps = w_ref.shape[0]
    for slot, i in enumerate(lines):
        if i < OWN:
            row = x_ref[2 * i + flip * (LINES - 1 - 4 * i)]
        else:
            at = i - lines[0]
            row = x_ref[at + flip * (len(lines) - 1 - 2 * at)]
        xp[slot, 0:8, :] = jnp.zeros((8, xp.shape[2]), xp.dtype)
        xp[slot, pixels + 8 :, :] = jnp.zeros((8, xp.shape[2]), xp.dtype)
        xp[slot, 8 : pixels + 8, :] = row
    for m in range(0, pixels, block):
        lefts = [
            jnp.concatenate(
                [xp[slot, m + 4 + 2 * j : m + 4 + 2 * j + block, :] for j in range(taps)], axis=1
            )
            for slot in range(len(lines))
        ]
        for o in touched(lines):
            acc = held[before.index(o), m : m + block, :] if o in before else None
            for slot, i in enumerate(lines):
                d = i - o + 2
                if 0 <= d <= 4:
                    part = jnp.dot(
                        lefts[slot], w_ref[d + flip * (4 - 2 * d)], preferred_element_type=F32
                    )
                    acc = part if acc is None else acc + part
            if o in done:
                hidden = jax.nn.gelu(acc, approximate=True).astype(BF)
                near = lax.dot_general(
                    h_ref[...], hidden, (((1,), (1,)), ((), ())), preferred_element_type=F32
                )
                near_ref[done.index(o), :, m : m + block] = near.astype(BF)
            else:
                outputs[1][later.index(o), m : m + block, :] = acc


def conv_stage(stage, flip, rows, weights, head, held):
    lines, done = STAGES[stage]
    pixels, channels = rows.shape[1:]
    before = [o for o in touched(STAGES[stage - 1][0]) if o not in STAGES[stage - 1][1]] if stage else []
    later = [o for o in touched(lines) if o not in done]
    out_shape = [jax.ShapeDtypeStruct((len(done), head.shape[0], pixels), BF)]
    if later:
        out_shape.append(jax.ShapeDtypeStruct((len(later), pixels, channels), F32))
    terms = sum(abs(i - o) <= 2 for i in lines for o in range(LINES))
    vmem = pl.BlockSpec(memory_space=pltpu.VMEM)
    out = pl.pallas_call(
        functools.partial(conv_kernel, lines, done, before, pixels, pixels),
        out_shape=out_shape,
        in_specs=[pl.BlockSpec(memory_space=pltpu.SMEM)] + [vmem] * (3 + len(held)),
        out_specs=[vmem] * len(out_shape),
        scratch_shapes=[pltpu.VMEM((len(lines), pixels + 16, channels), BF)],
        compiler_params=pltpu.CompilerParams(vmem_limit_bytes=24 << 20),
        cost_estimate=pl.CostEstimate(
            flops=4 * terms * pixels * weights.shape[1] * channels,
            bytes_accessed=4 << 20,
            transcendentals=len(done) * pixels * channels,
        ),
        name="conv_stage",
    )(flip, rows, weights, head, *held)
    return out[0], list(out[1:])


def socs_kernel(block, fields, last, weight_ref, place_ref, order_ref, first_ref, second_ref, *refs):
    field_refs, o_ref = refs[:fields], refs[-1]
    held = refs[fields:-1]
    pixels = field_refs[0].shape[2]
    left = [f[z + p] for p in (0, 1) for f in field_refs for z in range(0, f.shape[0], 2)]
    left = jnp.concatenate(left, axis=0)
    rows = left.shape[0] // 2
    order = order_ref[...]
    size = order.shape[0]
    step = size // ANG
    for n in range(0, pixels, block):
        cols = slice(n, n + block)
        total = jnp.zeros((rows, block), F32)
        for g_ref in (first_ref, second_ref):
            by_re = jnp.dot(left, g_ref[:, cols], preferred_element_type=F32)
            by_im = jnp.dot(left, g_ref[:, pixels + n : pixels + n + block], preferred_element_type=F32)
            re = by_re[:rows] - by_im[rows:]
            im = by_im[:rows] + by_re[rows:]
            total += re * re + im * im
        total = (total * weight_ref[place_ref[0]]).astype(BF)
        if not last:
            if rows >= size:
                own = jnp.dot(order, total[:size], preferred_element_type=F32)
                o_ref[:size, cols] = own.astype(BF)
                o_ref[size:, cols] = total[size:]
            else:
                o_ref[:, cols] = total
        else:
            low = place_ref[1]
            own = held[0][:size, cols].astype(F32)
            other = jnp.concatenate([held[0][size:, cols], held[1][:, cols], total], axis=0)
            other = jnp.dot(order, other, preferred_element_type=F32)
            for g in range(ANG):
                o_ref[g, low, :, cols] = own[g * step : (g + 1) * step].astype(BF)
                o_ref[g, 1 - low, :, cols] = other[g * step : (g + 1) * step].astype(BF)


def socs_image(weights, place, order, first, second, fields, held=()):
    pixels = fields[0].shape[2]
    rows = sum(f.shape[0] * f.shape[1] for f in fields) // 2
    scalar = pl.BlockSpec(memory_space=pltpu.SMEM)
    vmem = pl.BlockSpec(memory_space=pltpu.VMEM)
    if held:
        out_shape = jax.ShapeDtypeStruct((ANG, 2, order.shape[0] // ANG, pixels), BF)
    else:
        out_shape = jax.ShapeDtypeStruct((rows, pixels), BF)
    return pl.pallas_call(
        functools.partial(socs_kernel, 512, len(fields), bool(held)),
        out_shape=out_shape,
        in_specs=[scalar, scalar] + [vmem] * (3 + len(fields) + len(held)),
        out_specs=vmem,
        compiler_params=pltpu.CompilerParams(vmem_limit_bytes=20 << 20),
        cost_estimate=pl.CostEstimate(
            flops=16 * rows * pixels * pixels, bytes_accessed=9 << 20, transcendentals=0
        ),
        name="socs_image",
    )(weights, place, order, first, second, *fields, *held)


def resident_kernel(first_ref, second_ref, a_ref, b_ref, sems):
    parts = sems.shape[1]
    rows = a_ref.shape[0] // parts
    copies = [
        pltpu.make_async_copy(
            source.at[i * rows : (i + 1) * rows], target.at[i * rows : (i + 1) * rows], sems.at[k, i]
        )
        for i in range(parts)
        for k, (source, target) in enumerate(((first_ref, a_ref), (second_ref, b_ref)))
    ]
    for copy in copies:
        copy.start()
    for copy in copies:
        copy.wait()


def resident(first, second):
    return pl.pallas_call(
        resident_kernel,
        out_shape=[jax.ShapeDtypeStruct(first.shape, first.dtype)] * 2,
        in_specs=[pl.BlockSpec(memory_space=pl.ANY)] * 2,
        out_specs=[pl.BlockSpec(memory_space=pltpu.VMEM)] * 2,
        scratch_shapes=[pltpu.SemaphoreType.DMA((2, 8))],
        compiler_params=pltpu.CompilerParams(vmem_limit_bytes=12 << 20),
        cost_estimate=pl.CostEstimate(flops=0, bytes_accessed=4 * first.size * 2, transcendentals=0),
        name="resident",
    )(first, second)


def on_device(features, conv_weight, head_weight, kernels, source_weights):
    rows, pixels, channels = features.shape[1:]
    angle = lax.axis_index(("y", "xh"))
    section = lax.axis_index("s")
    depth = lax.axis_size("z")
    window = features[0]
    pairs = window.reshape(rows // 2, 2, pixels, channels)

    def halo(start, count):
        block = lax.dynamic_slice(pairs, (start, 1 - section, 0, 0), (count, 1, pixels, channels))
        return lax.ppermute(block[:, 0], "s", SWAP)

    first = halo(1 - section, 2)
    last = halo(2 * section, 1)
    mine = kernels[0]
    flip = section.astype(jnp.int32).reshape(1)
    taps = conv_weight.reshape(conv_weight.shape[0], -1, channels)
    head = head_weight.T
    near, held = [], []
    for stage, read in enumerate((window, first, last)):
        done, held = conv_stage(stage, flip, read, taps, head, held)
        near.append(done)
        if stage == 2:
            sibling = lax.ppermute(lax.optimization_barrier((mine, done))[0], "c", SWAP)
    near = jnp.concatenate(near, axis=0).reshape(LINES, ANG, 2, pixels).transpose(1, 2, 0, 3)
    at = lax.axis_index("z").astype(jnp.uint32)
    starts = [2 * ((at + k) % depth) for k in range(1, depth)]
    order = np.eye(ANG * depth * LINES).reshape(depth, LINES, ANG, -1).transpose(2, 0, 1, 3)
    order = order.reshape(ANG * depth * LINES, -1)
    width = LINES * ANG
    shifted = jnp.asarray(np.concatenate([order, order], axis=1).reshape(-1, 2 * depth, width).transpose(1, 0, 2), BF)
    shifted = lax.dynamic_slice_in_dim(shifted, at, depth, 0).transpose(1, 0, 2).reshape(order.shape)
    order = jnp.asarray(order, BF)
    place = jnp.stack([angle, lax.axis_index("xl")]).astype(jnp.int32)
    stays = section == 0
    near, starts, shifted, place, stays = lax.optimization_barrier((near, starts, shifted, place, stays))
    near = lax.all_to_all(near, ("y", "xh"), 0, 0, tiled=True)
    near = near.transpose(1, 2, 0, 3).reshape(2, LINES * ANG, pixels)
    early = lax.ppermute(near, "xl", SWAP)
    own = lax.all_gather(near, "z", axis=0, tiled=True)
    own, early = lax.optimization_barrier((own, early))
    ahead = [lax.dynamic_slice_in_dim(own, start, 2, 0) for start in starts]
    other_a = lax.ppermute(jnp.concatenate(ahead[:2], axis=0), "xl", SWAP)
    other_b = lax.ppermute(ahead[2], "xl", SWAP)
    mine, sibling = resident(mine, sibling)
    held_a = socs_image(source_weights, place, order, mine, sibling, [own, early])
    held_b = socs_image(source_weights, place, order, mine, sibling, [other_a])
    images = socs_image(source_weights, place, shifted, mine, sibling, [other_b], (held_a, held_b))
    images = images.reshape(2 * ANG, depth * LINES, pixels)
    pieces = lax.all_to_all(images, ("y", "xh", "xl"), 0, 0, tiled=True)
    total = jnp.sum(pieces.astype(F32), axis=0).reshape(depth, 2, OWN, pixels)
    kept, given = total[:, 0], total[:, 1]
    total = jnp.stack([jnp.where(stays, kept, given), jnp.where(stays, given, kept)])
    total = total.reshape(2 * depth, OWN * pixels // 128, 128)
    total = lax.all_to_all(total, ("s", "z"), 0, 0, tiled=True)
    even, odd = jnp.sum(total.reshape(2, depth, OWN, pixels // 128, 128), axis=1)
    return jnp.stack([even, odd[::-1]], axis=1).reshape(1, LINES, pixels)


def solution(mesh):
    fine = Mesh(mesh.devices.reshape(2, 4, 2, 2, 4, 2), ("s",) + TILE)
    in_specs = (P(TILE, "s", None, None), P(), P(), P(TILE, None, None), P())
    return jax.shard_map(
        on_device, mesh=fine, in_specs=in_specs, out_specs=P(TILE, "s", None), check_vma=False
    )
```
